128 devices in a mesh: gx: 16 (over y, x), gy: 8 (over z, core).
Axes of the slice: x: 4, y: 4, z: 4, core: 2. Of those that a mesh axis runs over, the one named last changes fastest.
Arguments:
- velocity: float32 [3, 128, 128, 128], P(None, 'gx', 'gy'), may hold values from -6 to 6
- marker_force: float32 [3, 16384, 128], P(None, ('gx', 'gy')), may hold values from -6 to 6
- marker_cell: int32 [16384, 128], P(('gx', 'gy')), may hold values from 0 to 16383
- block_brick: int32 [16384, 1], P(('gx', 'gy')), may hold values from 0 to 127; in each aligned block of 128 rows (0 to 127, 128 to 255, ...) at most 2 rows name the same one
Outputs:
- velocity_new: float32 [3, 128, 128, 128], P(None, 'gx', 'gy')
- marker_velocity: float32 [3, 16384, 128], P(None, ('gx', 'gy'))
The draws below stay inside these ranges and needn't reach their ends.
Inputs may be any that keep to these rules, and one draw needn't show every extreme that they name: `block_brick`: among the 128 blocks of one device no brick is named by more than 2 blocks, and some device names some brick exactly 2 times.
All inputs are finite; a program needn't handle non-finite values.
Results may differ from the reference program's by a relative error of at most 0.0003.
Values sent between devices are 32-bit elements; how exact they have to be, the bound alone decides.
No kernel may reach another device: no remote copies, remote signals or barrier semaphores. Data moves between devices by JAX's collectives and lax.ppermute only.
A program may use at most 128 MiB of HBM per device.

```python
import math
import jax
import jax.numpy as jnp
import numpy as np
from jax import lax

CX = 8
CY = 16
CZ = 128
MB = 128
MARK = 128
SWEEPS = 4
STEPS = 2
CAP = 2
NX = 128
NY = 128
BLOCKS = 16384
N_GY = 8
DEVICES = 128


def place_ends(array, rng, least, largest):
    index_at = [jax.random.randint(jax.random.fold_in(rng, axis), (), 0, length) for axis, length in enumerate(array.shape)]
    widest = array.shape.index(max(array.shape))
    next_to = index_at[:widest] + [(index_at[widest] + 1) % array.shape[widest]] + index_at[widest + 1:]
    return array.at[tuple(index_at)].set(least).at[tuple(next_to)].set(largest)


def steps_of(own_key, shape, cuts, low, top_value):
    level, own = 1.0, jax.random.fold_in(own_key, 6)
    for dim, shards_of in cuts:
        steps = jnp.exp(jax.random.uniform(jax.random.fold_in(own, dim), (shards_of,), jnp.float32, low / len(cuts), top_value / len(cuts)))
        level = level * jnp.repeat(steps, shape[dim] // shards_of).reshape([-1 if axis == dim else 1 for axis in range(len(shape))])
    return level


def assign_block(rng, own, number, rows, amount, top, most, lean):
    order = jax.random.permutation(rng, amount)
    packed, common = portions_of(amount, rows * top, most, lean, True), portions_of(amount, rows * top, most, lean, False)
    places = jnp.arange(amount)

    def named(sizes, turn):
        used = int((sizes > 0).sum())
        fixed = max(1, used // 4)
        passed = fixed + (places - fixed + turn * (used - fixed)) % max(1, amount - fixed)
        return jnp.zeros((amount,), jnp.int32).at[order[jnp.where(places < fixed, places, passed)]].set(jnp.asarray(sizes, jnp.int32))

    sizes = jnp.where(number % 4 == 0, named(packed, number // 4), named(common, number - number // 4 - 1))
    mixed = jax.random.permutation(jax.random.fold_in(own, 3), amount)
    donor, sink = mixed[0:amount // 2 * 2:2], mixed[1:amount // 2 * 2:2]
    margin = jnp.minimum(sizes[donor] - 1, most - sizes[sink]) // 2
    margin = jnp.where((donor == order[0]) | (sink == order[0]) | (sizes[sink] == 0), 0, jnp.maximum(margin, 0))
    passed = jax.random.randint(jax.random.fold_in(own, 4), (amount // 2,), 0, 1 << 20) % (margin + 1)
    sizes = sizes.at[donor].add(-passed).at[sink].add(passed)
    members = jnp.searchsorted(jnp.cumsum(sizes), jnp.arange(rows * top), side="right").astype(jnp.int32)
    grid = members.reshape(top, rows).T
    grid = grid[jax.random.permutation(jax.random.fold_in(own, 1), rows)]
    turn = jax.random.randint(jax.random.fold_in(own, 2), (rows, 1), 0, top)
    return jnp.take_along_axis(grid, (jnp.arange(top)[None, :] + turn) % top, axis=1)


def portions_of(amount, total, reach, lean, full):
    weights = [(1 << 20) // math.isqrt(rank ** lean) + 1 for rank in range(1, amount + 1)]
    largest = reach if full else min(reach, max(-(-total // amount), total * weights[0] // sum(weights)))
    least = 1 if total - largest >= amount - 1 else 0
    holding, rest = [largest] + [least] * (amount - 1), total - largest - least * (amount - 1)
    while rest > 0:
        candidates = [i for i in range(1, amount) if holding[i] < largest] or [i for i in range(1, amount) if holding[i] < reach]
        mass, remaining = sum([weights[i] for i in candidates]), rest
        for i in candidates:
            addition = min(reach - holding[i], max(1, remaining * weights[i] // mass), rest)
            holding[i] = holding[i] + addition
            rest = rest - addition
    return np.array(holding)


def bell_draw(rng, shape, deviation, bound, shards=(), kind=jnp.bfloat16):
    level = steps_of(rng, shape, shards, -0.22, 0.18) if shards else 1.0
    drawn = jax.random.normal(rng, shape, jnp.float32) * deviation * level
    return jnp.minimum(jnp.maximum(drawn, -bound), bound).astype(kind)


def setup_inputs(seed: int = 0) -> dict:
    keys = jax.random.split(jax.random.key(seed), 5)
    velocity = bell_draw(keys[0], (3, NX, NY, CZ), 1.0, 6.0, ((1, 16), (2, 8)), jnp.float32)
    marker_force = bell_draw(keys[1], (3, BLOCKS, MARK), 1.0, 6.0, ((1, 128),), jnp.float32)
    marker_cell = place_ends(jax.random.randint(keys[2], (BLOCKS, MARK), 0, CX * CY * CZ), jax.random.fold_in(keys[2], 1), 0, (CX * CY * CZ) - 1).astype(jnp.int32)
    block_brick_keys = jax.random.split(jax.random.fold_in(keys[3], 1), BLOCKS // MB)
    block_brick_turns = jax.random.permutation(jax.random.fold_in(keys[3], 3), BLOCKS // MB)
    block_brick = jax.vmap(lambda own, number: assign_block(jax.random.fold_in(keys[3], 2), own, number, MB, DEVICES, 1, CAP, 2))(block_brick_keys, block_brick_turns).reshape((BLOCKS, 1))
    return dict(velocity=velocity, marker_force=marker_force, marker_cell=marker_cell, block_brick=block_brick)


time_step = 0.5
viscosity = 0.2
stiffness = 1.0


def neighbours(grid_field):
    padded = jnp.pad(grid_field, [(0, 0)] * (grid_field.ndim - 3) + [(1, 1)] * 3)
    total_sum = padded[..., 2:, 1:-1, 1:-1] + padded[..., :-2, 1:-1, 1:-1]
    total_sum = total_sum + padded[..., 1:-1, 2:, 1:-1] + padded[..., 1:-1, :-2, 1:-1]
    return total_sum + padded[..., 1:-1, 1:-1, 2:] + padded[..., 1:-1, 1:-1, :-2]


def central(grid_field, direction):
    position = grid_field.ndim - 3 + direction
    widths = [(0, 0)] * grid_field.ndim
    widths[position] = (1, 1)
    padded = jnp.pad(grid_field, widths)
    length = padded.shape[position]
    forward = lax.slice_in_dim(padded, 2, length, axis=position)
    behind = lax.slice_in_dim(padded, 0, length - 2, axis=position)
    return 0.5 * (forward - behind)


def reference(velocity, marker_force, marker_cell, block_brick):
    size_x, size_y, size_z = velocity.shape[1], velocity.shape[2], velocity.shape[3]
    dest_brick = block_brick[:, 0]
    brick_x = dest_brick // N_GY
    brick_y = dest_brick % N_GY
    cell_x = marker_cell // (CY * CZ)
    cell_y = (marker_cell // CZ) % CY
    cell_z = marker_cell % CZ
    global_x = brick_x[:, None] * CX + cell_x
    global_y = brick_y[:, None] * CY + cell_y
    flat_cell = ((global_x * size_y + global_y) * size_z + cell_z).reshape(-1).astype(jnp.int32)
    force_now = marker_force.reshape(3, -1)
    current = velocity
    picked = force_now
    for step_number in range(STEPS):
        spread = jnp.zeros((3, size_x * size_y * size_z), current.dtype).at[:, flat_cell].add(force_now)
        spread = spread.reshape(current.shape)
        provisional = current + time_step * (viscosity * (neighbours(current) - 6.0 * current) + spread)
        source = (central(provisional[0], 0) + central(provisional[1], 1) + central(provisional[2], 2)) / time_step
        pressure = jnp.zeros_like(source)
        for sweep_number in range(SWEEPS):
            pressure = (neighbours(pressure) - source) / 6.0
        slope = jnp.stack([central(pressure, 0), central(pressure, 1), central(pressure, 2)])
        current = provisional - time_step * slope
        picked = current.reshape(3, -1)[:, flat_cell]
        if step_number + 1 < STEPS:
            force_now = force_now - stiffness * picked
    return current, picked.reshape(marker_force.shape)
```

```python
import jax
import jax.numpy as jnp
from jax import lax
from jax.experimental import pallas as pl
from jax.experimental.pallas import tpu as pltpu
from jax.sharding import PartitionSpec as P


F32 = jnp.float32
BF16 = jnp.bfloat16
VMEM = pltpu.VMEM
SMEM = pltpu.SMEM


def pack_kernel(bb, force, cell, out, tgt, cnt):
    devices = out.shape[0]
    blocks = force.shape[1]
    sub = lax.broadcasted_iota(jnp.int32, out.shape, 1)
    out[...] = jnp.where(sub % 4 == 3, -1.0, 0.0)

    def clear(i, carry):
        cnt[i] = 0
        return carry

    lax.fori_loop(0, devices, clear, 0, unroll=8)

    def one(m, carry):
        d = bb[m]
        e = cnt[d]
        cnt[d] = e + 1
        tgt[m] = 2 * d + e
        base = 4 * e
        for c in range(3):
            out[d, pl.ds(base + c, 1), :] = force[c, pl.ds(m, 1), :]
        out[d, pl.ds(base + 3, 1), :] = cell[pl.ds(m, 1), :].astype(F32)
        return carry

    lax.fori_loop(0, blocks, one, 0, unroll=4)


def pack(block_brick, force, cell, devices):
    blocks, width = cell.shape
    return pl.pallas_call(
        pack_kernel,
        out_shape=(
            jax.ShapeDtypeStruct((devices, 8, width), F32),
            jax.ShapeDtypeStruct((blocks,), jnp.int32),
        ),
        in_specs=[
            pl.BlockSpec(memory_space=SMEM),
            pl.BlockSpec(memory_space=VMEM),
            pl.BlockSpec(memory_space=VMEM),
        ],
        out_specs=(pl.BlockSpec(memory_space=VMEM), pl.BlockSpec(memory_space=SMEM)),
        scratch_shapes=[SMEM((devices,), jnp.int32)],
        name="pack",
    )(block_brick, force, cell)


def unpack_kernel(tgt, back, out):
    blocks = out.shape[1]

    def one(m, carry):
        t = tgt[m]
        d = t // 2
        base = 4 * (t % 2)
        for c in range(3):
            out[c, pl.ds(m, 1), :] = back[d, pl.ds(base + c, 1), :]
        return carry

    lax.fori_loop(0, blocks, one, 0, unroll=4)


def unpack(tgt, back, blocks):
    return pl.pallas_call(
        unpack_kernel,
        out_shape=jax.ShapeDtypeStruct((3, blocks, back.shape[2]), F32),
        in_specs=[pl.BlockSpec(memory_space=SMEM), pl.BlockSpec(memory_space=VMEM)],
        out_specs=pl.BlockSpec(memory_space=VMEM),
        name="unpack",
    )(tgt, back)


def zshift(v, lane):
    size = v.shape[-1]
    up = jnp.where(lane == size - 1, 0.0, pltpu.roll(v, size - 1, v.ndim - 1))
    down = jnp.where(lane == 0, 0.0, pltpu.roll(v, 1, v.ndim - 1))
    return up, down


def edge_flags():
    gx, gy = lax.axis_index("gx"), lax.axis_index("gy")
    nx, ny = lax.axis_size("gx"), lax.axis_size("gy")
    return gx > 0, gx < nx - 1, gy > 0, gy < ny - 1


CHUNK = 8


def split(v):
    hi = v.astype(BF16)
    lo = (v - hi.astype(F32)).astype(BF16)
    return hi, lo


def build(arrived, first, lhs, rhs, iota_r, iota_c):
    zero = jnp.zeros((), BF16)
    for s in range(CHUNK):
        packet = arrived[first + s]
        number = packet.astype(jnp.int32)
        row = ((number >> 13) * 128 + (number & 127)).astype(F32)
        col = ((number >> 7) & 63).astype(F32)
        hi = packet.astype(BF16).astype(F32)
        lo = packet - hi
        for e in range(2):
            k = (2 * s + e) * 128
            q = 4 * e + 3
            rr = jnp.broadcast_to(row[q : q + 1], (256, 128)).astype(BF16)
            rhs[:, k : k + 128] = jnp.where(iota_r == rr, 1.0, 0.0).astype(BF16)
            cc = jnp.broadcast_to(col[q : q + 1], (64, 128)).astype(BF16)
            mask = iota_c == cc
            for c in range(3):
                p = 4 * e + c
                for part, src in ((0, hi), (1, lo)):
                    val = jnp.broadcast_to(src[p : p + 1], (64, 128)).astype(BF16)
                    j = (2 * c + part) * 64
                    lhs[j : j + 64, k : k + 128] = jnp.where(mask, val, zero)
            lhs[384:448, k : k + 128] = jnp.where(mask, 1.0, 0.0).astype(BF16)


def spread_kernel(arrived, vel, xlo, xhi, ylo, yhi, prov, elo, ehi, spread, lhs0, rhs0, lhs1, rhs1, acc):
    senders = arrived.shape[0]
    iota_r = lax.broadcasted_iota(jnp.int32, (256, 128), 0).astype(F32).astype(BF16)
    iota_c = lax.broadcasted_iota(jnp.int32, (64, 128), 0).astype(F32).astype(BF16)
    dims = (((1,), (1,)), ((), ()))

    def mm(lhs, rhs):
        acc[...] += lax.dot_general(lhs[...], rhs[...], dims, preferred_element_type=F32)

    acc[...] = jnp.zeros_like(acc)
    steps = senders // (2 * CHUNK)
    build(arrived, 0, lhs0, rhs0, iota_r, iota_c)

    def loop(i, carry):
        build(arrived, (2 * i + 1) * CHUNK, lhs1, rhs1, iota_r, iota_c)
        mm(lhs0, rhs0)
        nxt = jnp.minimum((2 * i + 2) * CHUNK, senders - CHUNK)
        build(arrived, nxt, lhs0, rhs0, iota_r, iota_c)
        mm(lhs1, rhs1)
        return carry

    lax.fori_loop(0, steps, loop, 0)
    for c in range(3):
        total = acc[128 * c : 128 * c + 64] + acc[128 * c + 64 : 128 * c + 128]
        spread[c, 0:4] = total[:, :128].reshape(4, 16, 128)
        spread[c, 4:8] = total[:, 128:].reshape(4, 16, 128)
    spread[3, 0:4] = acc[384:448, :128].reshape(4, 16, 128)
    spread[3, 4:8] = acc[384:448, 128:].reshape(4, 16, 128)
    has_xlo, has_xhi, has_ylo, has_yhi = edge_flags()
    lane = lax.broadcasted_iota(jnp.int32, (16, 128), 1)
    sub = lax.broadcasted_iota(jnp.int32, (16, 128), 0)
    depth = elo.shape[1]
    nx = vel.shape[1]
    for c in range(3):
        for x in range(nx):
            here = vel[c, x]
            before = vel[c, x - 1] if x else jnp.where(has_xlo, xlo[c], 0.0)
            after = vel[c, x + 1] if x < nx - 1 else jnp.where(has_xhi, xhi[c], 0.0)
            left = jnp.broadcast_to(jnp.where(has_ylo, ylo[c, x : x + 1], 0.0), (16, 128))
            right = jnp.broadcast_to(jnp.where(has_yhi, yhi[c, x : x + 1], 0.0), (16, 128))
            ym = jnp.where(sub == 0, left, pltpu.roll(here, 1, 0))
            yp = jnp.where(sub == 15, right, pltpu.roll(here, 15, 0))
            up, down = zshift(here, lane)
            total = ((after + before) + (yp + ym)) + (up + down)
            value = here + 0.5 * (0.2 * (total - 6.0 * here) + spread[c, x])
            prov[c, x] = value
            if x < depth:
                elo[c, x] = value
            if x >= nx - depth:
                ehi[c, x - (nx - depth)] = value


def spread_call(arrived, vel, xlo, xhi, ylo, yhi, depth):
    _, nx, ny, nz = vel.shape
    k = CHUNK * 256
    return pl.pallas_call(
        spread_kernel,
        out_shape=(
            jax.ShapeDtypeStruct(vel.shape, F32),
            jax.ShapeDtypeStruct((3, depth, ny, nz), F32),
            jax.ShapeDtypeStruct((3, depth, ny, nz), F32),
            jax.ShapeDtypeStruct((4, nx, ny, nz), F32),
        ),
        in_specs=[pl.BlockSpec(memory_space=VMEM)] * 6,
        out_specs=(pl.BlockSpec(memory_space=VMEM),) * 4,
        scratch_shapes=[
            VMEM((448, k), BF16),
            VMEM((256, k), BF16),
            VMEM((448, k), BF16),
            VMEM((256, k), BF16),
            VMEM((448, 256), F32),
        ],
        name="spread",
    )(arrived, vel, xlo, xhi, ylo, yhi)


def rows_of(ref, lo, hi, c, i, depth, has_lo, has_hi):
    nx = ref.shape[1]
    if i < depth:
        return jnp.where(has_lo, lo[c, i], 0.0)
    if i < depth + nx:
        return ref[c, i - depth]
    return jnp.where(has_hi, hi[c, i - depth - nx], 0.0)


def edges_kernel(prov, xlo, xhi, source, tolow, tohigh):
    depth = xlo.shape[1]
    rows = source.shape[0]
    has_xlo, has_xhi, _, _ = edge_flags()
    lane = lax.broadcasted_iota(jnp.int32, (16, 128), 1)
    sub = lax.broadcasted_iota(jnp.int32, (16, 128), 0)
    sub8 = lax.broadcasted_iota(jnp.int32, (8, 128), 0)

    def row(c, i):
        return rows_of(prov, xlo, xhi, c, i, depth, has_xlo, has_xhi)

    for j in range(rows):
        i = j + 1
        p0, p1, p2 = row(0, i), row(1, i), row(2, i)
        ym = jnp.where(sub == 0, 0.0, pltpu.roll(p1, 1, 0))
        yp = jnp.where(sub == 15, 0.0, pltpu.roll(p1, 15, 0))
        up, down = zshift(p2, lane)
        value = (row(0, i + 1) - row(0, i - 1)) + (yp - ym) + (up - down)
        source[j] = value
        high, low = value[8:16], value[0:8]
        for c, p in enumerate((p0, p1, p2)):
            high = jnp.where(sub8 == c, pltpu.roll(p[8:16], c + 1, 0), high)
            low = jnp.where(sub8 == 5 + c, pltpu.roll(p[0:8], 5 + c, 0), low)
        tohigh[j] = high
        tolow[j] = low


def edges_call(prov, xlo, xhi):
    _, nx, ny, nz = prov.shape
    rows = nx + 2 * xlo.shape[1] - 2
    return pl.pallas_call(
        edges_kernel,
        out_shape=(
            jax.ShapeDtypeStruct((rows, ny, nz), F32),
            jax.ShapeDtypeStruct((rows, 8, nz), F32),
            jax.ShapeDtypeStruct((rows, 8, nz), F32),
        ),
        in_specs=[pl.BlockSpec(memory_space=VMEM)] * 3,
        out_specs=(pl.BlockSpec(memory_space=VMEM),) * 3,
        name="edges",
    )(prov, xlo, xhi)


def solve(prov, xlo, xhi, source, fromlow, fromhigh, pa, pb):
    depth = xlo.shape[1]
    rows = source.shape[0]
    nx = prov.shape[1]
    has_xlo, has_xhi, has_ylo, has_yhi = edge_flags()
    sub = lax.broadcasted_iota(jnp.int32, (32, 128), 0)
    lane = lax.broadcasted_iota(jnp.int32, (32, 128), 1)
    inside = ((sub >= 8) | has_ylo) & ((sub < 24) | has_yhi)
    zero = jnp.zeros((8, 128), F32)
    halo = depth - 1

    def masked(v, j):
        keep = inside
        if j < halo:
            keep = inside & has_xlo
        elif j >= halo + nx:
            keep = inside & has_xhi
        return jnp.where(keep, v, 0.0)

    def row(c, j):
        return rows_of(prov, xlo, xhi, c, j + 1, depth, has_xlo, has_xhi)

    src = []
    for j in range(rows):
        lowp = fromlow[j]
        highp = fromhigh[j]
        p1 = row(1, j)
        low1 = jnp.where(has_ylo, lowp[1:2], 0.0)
        high1 = jnp.where(has_yhi, highp[6:7], 0.0)
        value = jnp.concatenate([lowp, source[j], highp], axis=0)
        add = jnp.where(sub == 7, jnp.broadcast_to(p1[0:1], (32, 128)), 0.0)
        add = jnp.where(sub == 8, jnp.broadcast_to(-low1, (32, 128)), add)
        add = jnp.where(sub == 23, jnp.broadcast_to(high1, (32, 128)), add)
        add = jnp.where(sub == 24, jnp.broadcast_to(-p1[15:16], (32, 128)), add)
        value = masked((value + add) * (1.0 / 6.0), j)
        src.append(value)
        pa[j] = -value
    cur, new = pa, pb
    for sweep in range(1, 4):
        for j in range(sweep, rows - sweep):
            here = cur[j]
            up, down = zshift(here, lane)
            total = (cur[j - 1] + cur[j + 1]) + (pltpu.roll(here, 1, 0) + pltpu.roll(here, 31, 0))
            total = total + (up + down)
            new[j] = masked(total * (1.0 / 6.0) - src[j], j)
        cur, new = new, cur
    return cur, halo, row


def step_kernel(prov, xlo, xhi, source, fromlow, fromhigh, spread, prov2, elo, ehi, pa, pb, ux):
    nx = prov.shape[1]
    depth2 = elo.shape[1]
    p, halo, row = solve(prov, xlo, xhi, source, fromlow, fromhigh, pa, pb)
    has_xlo, has_xhi, has_ylo, has_yhi = edge_flags()
    sub = lax.broadcasted_iota(jnp.int32, (32, 128), 0)
    lane = lax.broadcasted_iota(jnp.int32, (32, 128), 1)
    inside = ((sub >= 8) | has_ylo) & ((sub < 24) | has_yhi)
    for x in range(-1, nx + 1):
        j = x + halo
        here = p[j]
        up, down = zshift(here, lane)
        slopes = (
            p[j + 1] - p[j - 1],
            pltpu.roll(here, 31, 0) - pltpu.roll(here, 1, 0),
            up - down,
        )
        keep = inside
        if x < 0:
            keep = inside & has_xlo
        elif x >= nx:
            keep = inside & has_xhi
        lowp, highp = fromlow[j], fromhigh[j]
        for c in range(3):
            wide = jnp.concatenate(
                [pltpu.roll(lowp, 7 - c, 0), row(c, j), pltpu.roll(highp, 3 - c, 0)], axis=0
            )
            ux[c, x + 1] = jnp.where(keep, wide - 0.25 * slopes[c], 0.0)
    lane16 = lax.broadcasted_iota(jnp.int32, (16, 128), 1)
    for c in range(3):
        for x in range(nx):
            here = ux[c, x + 1]
            ys = pltpu.roll(here, 1, 0) + pltpu.roll(here, 31, 0)
            mid = here[8:24]
            up, down = zshift(mid, lane16)
            total = (ux[c, x, 8:24] + ux[c, x + 2, 8:24]) + ys[8:24] + (up + down)
            pull = spread[c, x] - spread[3, x] * mid
            value = mid + 0.5 * (0.2 * (total - 6.0 * mid) + pull)
            prov2[c, x] = value
            if x < depth2:
                elo[c, x] = value
            if x >= nx - depth2:
                ehi[c, x - (nx - depth2)] = value


def step_call(prov, xlo, xhi, source, fromlow, fromhigh, spread, depth2):
    _, nx, ny, nz = prov.shape
    rows = source.shape[0]
    return pl.pallas_call(
        step_kernel,
        out_shape=(
            jax.ShapeDtypeStruct(prov.shape, F32),
            jax.ShapeDtypeStruct((3, depth2, ny, nz), F32),
            jax.ShapeDtypeStruct((3, depth2, ny, nz), F32),
        ),
        in_specs=[pl.BlockSpec(memory_space=VMEM)] * 7,
        out_specs=(pl.BlockSpec(memory_space=VMEM),) * 3,
        scratch_shapes=[
            VMEM((rows, 32, nz), F32),
            VMEM((rows, 32, nz), F32),
            VMEM((3, nx + 2, 32, nz), F32),
        ],
        name="step",
    )(prov, xlo, xhi, source, fromlow, fromhigh, spread)


GROUP = 4


def last_kernel(prov, xlo, xhi, source, fromlow, fromhigh, arrived, vel, picked, pa, pb, table):
    nx = prov.shape[1]
    senders = arrived.shape[0]
    p, halo, row = solve(prov, xlo, xhi, source, fromlow, fromhigh, pa, pb)
    lane16 = lax.broadcasted_iota(jnp.int32, (16, 128), 1)
    for x in range(nx):
        j = x + halo
        here = p[j]
        mid = here[8:24]
        up, down = zshift(mid, lane16)
        slopes = (
            p[j + 1, 8:24] - p[j - 1, 8:24],
            (pltpu.roll(here, 31, 0) - pltpu.roll(here, 1, 0))[8:24],
            up - down,
        )
        for c in range(3):
            value = prov[c, x] - 0.25 * slopes[c]
            vel[c, x] = value
            hi, lo = split(value)
            r = 64 * c + 16 * (x % 4)
            k = 128 * (x // 4)
            table[r : r + 16, k : k + 128] = hi
            table[192 + r : 192 + r + 16, k : k + 128] = lo
    iota_r = lax.broadcasted_iota(jnp.int32, (256, 128), 0).astype(F32).astype(BF16)
    iota_c = lax.broadcasted_iota(jnp.int32, (64, 128), 0)
    tab = table[...]

    def loop(i, carry):
        hot = []
        cols = []
        for s in range(GROUP):
            packet = arrived[i * GROUP + s]
            number = packet.astype(jnp.int32)
            rowf = ((number >> 13) * 128 + (number & 127)).astype(F32)
            cols.append((number >> 7) & 63)
            for e in range(2):
                q = 4 * e + 3
                rr = jnp.broadcast_to(rowf[q : q + 1], (256, 128)).astype(BF16)
                hot.append(jnp.where(iota_r == rr, 1.0, 0.0).astype(BF16))
        for h in range(GROUP):
            got = jnp.dot(tab, jnp.concatenate(hot[2 * h : 2 * h + 2], axis=1), preferred_element_type=F32)
            for e in range(2):
                q = 4 * e + 3
                mask = iota_c == jnp.broadcast_to(cols[h][q : q + 1], (64, 128))
                for c in range(3):
                    k = 128 * e
                    val = got[64 * c : 64 * c + 64, k : k + 128] + got[192 + 64 * c : 256 + 64 * c, k : k + 128]
                    val = jnp.where(mask, val, 0.0)
                    picked[i * GROUP + h, 4 * e + c : 4 * e + c + 1, :] = jnp.sum(val, axis=0, keepdims=True)
                picked[i * GROUP + h, 4 * e + 3 : 4 * e + 4, :] = jnp.zeros((1, 128), F32)
        return carry

    lax.fori_loop(0, senders // GROUP, loop, 0)


def last_call(prov, xlo, xhi, source, fromlow, fromhigh, arrived):
    _, nx, ny, nz = prov.shape
    rows = source.shape[0]
    return pl.pallas_call(
        last_kernel,
        out_shape=(
            jax.ShapeDtypeStruct(prov.shape, F32),
            jax.ShapeDtypeStruct(arrived.shape, F32),
        ),
        in_specs=[pl.BlockSpec(memory_space=VMEM)] * 7,
        out_specs=(pl.BlockSpec(memory_space=VMEM),) * 2,
        scratch_shapes=[
            VMEM((rows, 32, nz), F32),
            VMEM((rows, 32, nz), F32),
            VMEM((384, 256), BF16),
        ],
        name="last",
    )(prov, xlo, xhi, source, fromlow, fromhigh, arrived)


def ring(value, axis, shift):
    count = lax.axis_size(axis)
    return lax.ppermute(value, axis, [(i, (i + shift) % count) for i in range(count)])


def exchange(value, axis):
    pass


def body(velocity, marker_force, marker_cell, block_brick):
    devices = lax.axis_size("gx") * lax.axis_size("gy")
    blocks = marker_cell.shape[0]
    axes = ("gx", "gy")
    xlo = ring(velocity[:, -1], "gx", 1)
    xhi = ring(velocity[:, 0], "gx", -1)
    ylo = ring(velocity[:, :, -1], "gy", 1)
    yhi = ring(velocity[:, :, 0], "gy", -1)
    outgoing, target = pack(block_brick.reshape(blocks), marker_force, marker_cell, devices)
    arrived = lax.all_to_all(outgoing, axes, split_axis=0, concat_axis=0, tiled=True)
    prov, elo, ehi, spread = spread_call(arrived, velocity, xlo, xhi, ylo, yhi, 6)
    hlo, hhi = ring(ehi, "gx", 1), ring(elo, "gx", -1)
    source, tolow, tohigh = edges_call(prov, hlo, hhi)
    fromlow, fromhigh = ring(tohigh, "gy", 1), ring(tolow, "gy", -1)
    prov, elo, ehi = step_call(prov, hlo, hhi, source, fromlow, fromhigh, spread, 5)
    hlo, hhi = ring(ehi, "gx", 1), ring(elo, "gx", -1)
    source, tolow, tohigh = edges_call(prov, hlo, hhi)
    fromlow, fromhigh = ring(tohigh, "gy", 1), ring(tolow, "gy", -1)
    final, picked = last_call(prov, hlo, hhi, source, fromlow, fromhigh, arrived)
    back = lax.all_to_all(picked, axes, split_axis=0, concat_axis=0, tiled=True)
    return final, unpack(target, back, blocks)


def solution(mesh):
    return jax.shard_map(
        body,
        mesh=mesh,
        in_specs=(
            P(None, "gx", "gy", None),
            P(None, ("gx", "gy"), None),
            P(("gx", "gy"), None),
            P(("gx", "gy"), None),
        ),
        out_specs=(P(None, "gx", "gy", None), P(None, ("gx", "gy"), None)),
        check_vma=False,
    )
```

```python
import jax
import jax.numpy as jnp
from jax import lax
from jax.experimental import pallas as pl
from jax.experimental.pallas import tpu as pltpu
from jax.sharding import PartitionSpec as P


F32 = jnp.float32
BF16 = jnp.bfloat16
VMEM = pltpu.VMEM
SMEM = pltpu.SMEM


def pack_kernel(bb, force, cell, out, tgt, cnt, comb):
    devices = out.shape[0]
    blocks = force.shape[1]
    sub = lax.broadcasted_iota(jnp.int32, out.shape, 1)
    out[...] = jnp.where(sub % 4 == 3, -1.0, 0.0)
    for k in range(0, blocks, 8):
        for c in range(3):
            comb[pl.ds(8 * k + c, 8, 8), :] = force[c, k : k + 8, :]
        comb[pl.ds(8 * k + 3, 8, 8), :] = cell[k : k + 8, :].astype(F32)

    def clear(i, carry):
        cnt[i] = 0
        return carry

    lax.fori_loop(0, devices, clear, 0, unroll=8)

    def one(m, carry):
        d = bb[m]
        e = cnt[d]
        cnt[d] = e + 1
        tgt[m] = 2 * d + e
        out[d, pl.ds(4 * e, 4), :] = comb[pl.ds(pl.multiple_of(8 * m, 8), 4), :]
        return carry

    lax.fori_loop(0, blocks, one, 0, unroll=8)


def pack(block_brick, force, cell, devices):
    blocks, width = cell.shape
    return pl.pallas_call(
        pack_kernel,
        out_shape=(
            jax.ShapeDtypeStruct((devices, 8, width), F32),
            jax.ShapeDtypeStruct((blocks,), jnp.int32),
        ),
        in_specs=[
            pl.BlockSpec(memory_space=SMEM),
            pl.BlockSpec(memory_space=VMEM),
            pl.BlockSpec(memory_space=VMEM),
        ],
        out_specs=(pl.BlockSpec(memory_space=VMEM), pl.BlockSpec(memory_space=SMEM)),
        scratch_shapes=[SMEM((devices,), jnp.int32), VMEM((8 * blocks, width), F32)],
        name="pack",
    )(block_brick, force, cell)


def unpack_kernel(tgt, back, out, comb):
    blocks = out.shape[1]

    def one(m, carry):
        t = tgt[m]
        d = t // 2
        comb[pl.ds(pl.multiple_of(8 * m, 8), 4), :] = back[d, pl.ds(4 * (t % 2), 4), :]
        return carry

    lax.fori_loop(0, blocks, one, 0, unroll=8)
    for k in range(0, blocks, 8):
        for c in range(3):
            out[c, k : k + 8, :] = comb[pl.ds(8 * k + c, 8, 8), :]


def unpack(tgt, back, blocks):
    return pl.pallas_call(
        unpack_kernel,
        out_shape=jax.ShapeDtypeStruct((3, blocks, back.shape[2]), F32),
        in_specs=[pl.BlockSpec(memory_space=SMEM), pl.BlockSpec(memory_space=VMEM)],
        out_specs=pl.BlockSpec(memory_space=VMEM),
        scratch_shapes=[VMEM((8 * blocks, back.shape[2]), F32)],
        name="unpack",
    )(tgt, back)


def zshift(v, lane):
    size = v.shape[-1]
    up = jnp.where(lane == size - 1, 0.0, pltpu.roll(v, size - 1, v.ndim - 1))
    down = jnp.where(lane == 0, 0.0, pltpu.roll(v, 1, v.ndim - 1))
    return up, down


def edge_flags():
    gx, gy = lax.axis_index("gx"), lax.axis_index("gy")
    nx, ny = lax.axis_size("gx"), lax.axis_size("gy")
    return gx > 0, gx < nx - 1, gy > 0, gy < ny - 1


CHUNK = 16


def split(v):
    hi = v.astype(BF16)
    lo = (v - hi.astype(F32)).astype(BF16)
    return hi, lo


def one_hots(packet, iota_r, iota_c):
    number = packet.astype(jnp.int32)
    row = ((number >> 13) * 128 + (number & 127)).astype(F32)
    col = ((number >> 7) & 63).astype(F32)
    hi = packet.astype(BF16).astype(F32)
    lo = packet - hi
    one, zero = jnp.ones((), BF16), jnp.zeros((), BF16)
    out = []
    for e in range(2):
        q = 4 * e + 3
        rr = jnp.broadcast_to(row[q : q + 1], (256, 128)).astype(BF16)
        hot = jnp.where(iota_r == rr, one, zero)
        cc = jnp.broadcast_to(col[q : q + 1], (64, 128)).astype(BF16)
        mask = iota_c == cc
        rows = []
        for c in range(3):
            p = 4 * e + c
            for src in (hi, lo):
                val = jnp.broadcast_to(src[p : p + 1], (64, 128)).astype(BF16)
                rows.append(jnp.where(mask, val, zero))
        rows.append(jnp.where(mask, one, zero))
        out.append((hot, jnp.concatenate(rows, axis=0)))
    return out


def spread_kernel(arrived, vel, xlo, xhi, ylo, yhi, prov, elo, ehi, spread, acc):
    senders = arrived.shape[0]
    iota_r = lax.broadcasted_iota(jnp.int32, (256, 128), 0).astype(F32).astype(BF16)
    iota_c = lax.broadcasted_iota(jnp.int32, (64, 128), 0).astype(F32).astype(BF16)
    dims = (((1,), (1,)), ((), ()))
    acc[...] = jnp.zeros_like(acc)

    def loop(i, carry):
        hots, vals = [], []
        for s in range(CHUNK):
            for hot, val in one_hots(arrived[i * CHUNK + s], iota_r, iota_c):
                hots.append(hot)
                vals.append(val)
        acc[...] += lax.dot_general(
            jnp.concatenate(vals, axis=1), jnp.concatenate(hots, axis=1), dims, preferred_element_type=F32
        )
        return carry

    lax.fori_loop(0, senders // CHUNK, loop, 0)
    for c in range(3):
        total = acc[128 * c : 128 * c + 64] + acc[128 * c + 64 : 128 * c + 128]
        spread[c, 0:4] = total[:, :128].reshape(4, 16, 128)
        spread[c, 4:8] = total[:, 128:].reshape(4, 16, 128)
    spread[3, 0:4] = acc[384:448, :128].reshape(4, 16, 128)
    spread[3, 4:8] = acc[384:448, 128:].reshape(4, 16, 128)
    has_xlo, has_xhi, has_ylo, has_yhi = edge_flags()
    lane = lax.broadcasted_iota(jnp.int32, (16, 128), 1)
    sub = lax.broadcasted_iota(jnp.int32, (16, 128), 0)
    depth = elo.shape[1]
    nx = vel.shape[1]
    for c in range(3):
        for x in range(nx):
            here = vel[c, x]
            before = vel[c, x - 1] if x else jnp.where(has_xlo, xlo[c], 0.0)
            after = vel[c, x + 1] if x < nx - 1 else jnp.where(has_xhi, xhi[c], 0.0)
            left = jnp.broadcast_to(jnp.where(has_ylo, ylo[c, x : x + 1], 0.0), (16, 128))
            right = jnp.broadcast_to(jnp.where(has_yhi, yhi[c, x : x + 1], 0.0), (16, 128))
            ym = jnp.where(sub == 0, left, pltpu.roll(here, 1, 0))
            yp = jnp.where(sub == 15, right, pltpu.roll(here, 15, 0))
            up, down = zshift(here, lane)
            total = ((after + before) + (yp + ym)) + (up + down)
            value = here + 0.5 * (0.2 * (total - 6.0 * here) + spread[c, x])
            prov[c, x] = value
            if x < depth:
                elo[c, x] = value
            if x >= nx - depth:
                ehi[c, x - (nx - depth)] = value


def spread_call(arrived, vel, xlo, xhi, ylo, yhi, depth):
    _, nx, ny, nz = vel.shape
    return pl.pallas_call(
        spread_kernel,
        out_shape=(
            jax.ShapeDtypeStruct(vel.shape, F32),
            jax.ShapeDtypeStruct((3, depth, ny, nz), F32),
            jax.ShapeDtypeStruct((3, depth, ny, nz), F32),
            jax.ShapeDtypeStruct((4, nx, ny, nz), F32),
        ),
        in_specs=[pl.BlockSpec(memory_space=VMEM)] * 6,
        out_specs=(pl.BlockSpec(memory_space=VMEM),) * 4,
        scratch_shapes=[VMEM((448, 256), F32)],
        name="spread",
    )(arrived, vel, xlo, xhi, ylo, yhi)


def rows_of(ref, lo, hi, c, i, depth, has_lo, has_hi):
    nx = ref.shape[1]
    if i < depth:
        return jnp.where(has_lo, lo[c, i], 0.0)
    if i < depth + nx:
        return ref[c, i - depth]
    return jnp.where(has_hi, hi[c, i - depth - nx], 0.0)


def edges_kernel(prov, xlo, xhi, source, tolow, tohigh):
    depth = xlo.shape[1]
    rows = source.shape[0]
    has_xlo, has_xhi, _, _ = edge_flags()
    lane = lax.broadcasted_iota(jnp.int32, (16, 128), 1)
    sub = lax.broadcasted_iota(jnp.int32, (16, 128), 0)
    sub8 = lax.broadcasted_iota(jnp.int32, (8, 128), 0)

    def row(c, i):
        return rows_of(prov, xlo, xhi, c, i, depth, has_xlo, has_xhi)

    for j in range(rows):
        i = j + 1
        p0, p1, p2 = row(0, i), row(1, i), row(2, i)
        ym = jnp.where(sub == 0, 0.0, pltpu.roll(p1, 1, 0))
        yp = jnp.where(sub == 15, 0.0, pltpu.roll(p1, 15, 0))
        up, down = zshift(p2, lane)
        value = (row(0, i + 1) - row(0, i - 1)) + (yp - ym) + (up - down)
        source[j] = value
        high, low = value[8:16], value[0:8]
        for c, p in enumerate((p0, p1, p2)):
            high = jnp.where(sub8 == c, pltpu.roll(p[8:16], c + 1, 0), high)
            low = jnp.where(sub8 == 5 + c, pltpu.roll(p[0:8], 5 + c, 0), low)
        tohigh[j] = high
        tolow[j] = low


def edges_call(prov, xlo, xhi):
    _, nx, ny, nz = prov.shape
    rows = nx + 2 * xlo.shape[1] - 2
    return pl.pallas_call(
        edges_kernel,
        out_shape=(
            jax.ShapeDtypeStruct((rows, ny, nz), F32),
            jax.ShapeDtypeStruct((rows, 8, nz), F32),
            jax.ShapeDtypeStruct((rows, 8, nz), F32),
        ),
        in_specs=[pl.BlockSpec(memory_space=VMEM)] * 3,
        out_specs=(pl.BlockSpec(memory_space=VMEM),) * 3,
        name="edges",
    )(prov, xlo, xhi)


def solve(prov, xlo, xhi, source, fromlow, fromhigh, pa, pb):
    depth = xlo.shape[1]
    rows = source.shape[0]
    nx = prov.shape[1]
    has_xlo, has_xhi, has_ylo, has_yhi = edge_flags()
    sub = lax.broadcasted_iota(jnp.int32, (32, 128), 0)
    lane = lax.broadcasted_iota(jnp.int32, (32, 128), 1)
    inside = ((sub >= 8) | has_ylo) & ((sub < 24) | has_yhi)
    zero = jnp.zeros((8, 128), F32)
    halo = depth - 1

    def masked(v, j):
        keep = inside
        if j < halo:
            keep = inside & has_xlo
        elif j >= halo + nx:
            keep = inside & has_xhi
        return jnp.where(keep, v, 0.0)

    def row(c, j):
        return rows_of(prov, xlo, xhi, c, j + 1, depth, has_xlo, has_xhi)

    src = []
    for j in range(rows):
        lowp = fromlow[j]
        highp = fromhigh[j]
        p1 = row(1, j)
        low1 = jnp.where(has_ylo, lowp[1:2], 0.0)
        high1 = jnp.where(has_yhi, highp[6:7], 0.0)
        value = jnp.concatenate([lowp, source[j], highp], axis=0)
        add = jnp.where(sub == 7, jnp.broadcast_to(p1[0:1], (32, 128)), 0.0)
        add = jnp.where(sub == 8, jnp.broadcast_to(-low1, (32, 128)), add)
        add = jnp.where(sub == 23, jnp.broadcast_to(high1, (32, 128)), add)
        add = jnp.where(sub == 24, jnp.broadcast_to(-p1[15:16], (32, 128)), add)
        value = masked((value + add) * (1.0 / 6.0), j)
        src.append(value)
        pa[j] = -value
    cur, new = pa, pb
    for sweep in range(1, 4):
        for j in range(sweep, rows - sweep):
            here = cur[j]
            up, down = zshift(here, lane)
            total = (cur[j - 1] + cur[j + 1]) + (pltpu.roll(here, 1, 0) + pltpu.roll(here, 31, 0))
            total = total + (up + down)
            new[j] = masked(total * (1.0 / 6.0) - src[j], j)
        cur, new = new, cur
    return cur, halo, row


def step_kernel(prov, xlo, xhi, source, fromlow, fromhigh, spread, prov2, elo, ehi, pa, pb, ux):
    nx = prov.shape[1]
    depth2 = elo.shape[1]
    p, halo, row = solve(prov, xlo, xhi, source, fromlow, fromhigh, pa, pb)
    has_xlo, has_xhi, has_ylo, has_yhi = edge_flags()
    sub = lax.broadcasted_iota(jnp.int32, (32, 128), 0)
    lane = lax.broadcasted_iota(jnp.int32, (32, 128), 1)
    inside = ((sub >= 8) | has_ylo) & ((sub < 24) | has_yhi)
    for x in range(-1, nx + 1):
        j = x + halo
        here = p[j]
        up, down = zshift(here, lane)
        slopes = (
            p[j + 1] - p[j - 1],
            pltpu.roll(here, 31, 0) - pltpu.roll(here, 1, 0),
            up - down,
        )
        keep = inside
        if x < 0:
            keep = inside & has_xlo
        elif x >= nx:
            keep = inside & has_xhi
        lowp, highp = fromlow[j], fromhigh[j]
        for c in range(3):
            wide = jnp.concatenate(
                [pltpu.roll(lowp, 7 - c, 0), row(c, j), pltpu.roll(highp, 3 - c, 0)], axis=0
            )
            ux[c, x + 1] = jnp.where(keep, wide - 0.25 * slopes[c], 0.0)
    lane16 = lax.broadcasted_iota(jnp.int32, (16, 128), 1)
    for c in range(3):
        for x in range(nx):
            here = ux[c, x + 1]
            ys = pltpu.roll(here, 1, 0) + pltpu.roll(here, 31, 0)
            mid = here[8:24]
            up, down = zshift(mid, lane16)
            total = (ux[c, x, 8:24] + ux[c, x + 2, 8:24]) + ys[8:24] + (up + down)
            pull = spread[c, x] - spread[3, x] * mid
            value = mid + 0.5 * (0.2 * (total - 6.0 * mid) + pull)
            prov2[c, x] = value
            if x < depth2:
                elo[c, x] = value
            if x >= nx - depth2:
                ehi[c, x - (nx - depth2)] = value


def step_call(prov, xlo, xhi, source, fromlow, fromhigh, spread, depth2):
    _, nx, ny, nz = prov.shape
    rows = source.shape[0]
    return pl.pallas_call(
        step_kernel,
        out_shape=(
            jax.ShapeDtypeStruct(prov.shape, F32),
            jax.ShapeDtypeStruct((3, depth2, ny, nz), F32),
            jax.ShapeDtypeStruct((3, depth2, ny, nz), F32),
        ),
        in_specs=[pl.BlockSpec(memory_space=VMEM)] * 7,
        out_specs=(pl.BlockSpec(memory_space=VMEM),) * 3,
        scratch_shapes=[
            VMEM((rows, 32, nz), F32),
            VMEM((rows, 32, nz), F32),
            VMEM((3, nx + 2, 32, nz), F32),
        ],
        name="step",
    )(prov, xlo, xhi, source, fromlow, fromhigh, spread)


DENSE, SPARSE = 11, 5


def last_kernel(prov, xlo, xhi, source, fromlow, fromhigh, arrived, vel, picked, pa, pb, table):
    nx = prov.shape[1]
    senders = arrived.shape[0]
    p, halo, row = solve(prov, xlo, xhi, source, fromlow, fromhigh, pa, pb)
    lane16 = lax.broadcasted_iota(jnp.int32, (16, 128), 1)
    for x in range(nx):
        j = x + halo
        here = p[j]
        mid = here[8:24]
        up, down = zshift(mid, lane16)
        slopes = (
            p[j + 1, 8:24] - p[j - 1, 8:24],
            (pltpu.roll(here, 31, 0) - pltpu.roll(here, 1, 0))[8:24],
            up - down,
        )
        for c in range(3):
            value = prov[c, x] - 0.25 * slopes[c]
            vel[c, x] = value
            hi, lo = split(value)
            r = 64 * c + 16 * (x % 4)
            k = 128 * (x // 4)
            table[r : r + 16, k : k + 128] = hi
            table[192 + r : 192 + r + 16, k : k + 128] = lo
    rows8 = lax.broadcasted_iota(jnp.int32, (8, 128), 0)
    iota_r = lax.broadcasted_iota(jnp.int32, (256, 128), 0).astype(F32).astype(BF16)
    iota_c = lax.broadcasted_iota(jnp.int32, (64, 128), 0)
    one, zero = jnp.ones((), BF16), jnp.zeros((), BF16)
    blank = jnp.zeros((1, 128), F32)

    def dense(first):
        hot, cols = [], []
        for s in range(DENSE):
            number = arrived[first + s].astype(jnp.int32)
            rowf = ((number >> 13) * 128 + (number & 127)).astype(F32)
            col = (number >> 7) & 63
            for e in range(2):
                q = 4 * e + 3
                rr = jnp.broadcast_to(rowf[q : q + 1], (256, 128)).astype(BF16)
                hot.append(jnp.where(iota_r == rr, one, zero))
                cols.append(col[q : q + 1])
        got = jnp.dot(table[...], jnp.concatenate(hot, axis=1), preferred_element_type=F32)
        for s in range(DENSE):
            for e in range(2):
                k = 128 * (2 * s + e)
                mask = iota_c == jnp.broadcast_to(cols[2 * s + e], (64, 128))
                for c in range(3):
                    val = got[64 * c : 64 * c + 64, k : k + 128] + got[192 + 64 * c : 256 + 64 * c, k : k + 128]
                    val = jnp.where(mask, val, 0.0)
                    picked[first + s, 4 * e + c : 4 * e + c + 1, :] = jnp.sum(val, axis=0, keepdims=True)
                picked[first + s, 4 * e + 3 : 4 * e + 4, :] = blank

    def sparse(first):
        for s in range(SPARSE):
            number = arrived[first + s].astype(jnp.int32)
            for e in range(2):
                q = 4 * e + 3
                cell = jnp.broadcast_to(number[q : q + 1], (8, 128))
                z = cell & 127
                column = (cell >> 7) - rows8
                acc = [jnp.zeros((8, 128), F32) for _ in range(3)]
                for g in range(2 * nx):
                    mask = column == 8 * g
                    for c in range(3):
                        field = vel[c, g // 2, 8 * (g % 2) : 8 * (g % 2) + 8, :]
                        got = jnp.take_along_axis(field, z, axis=1, mode="promise_in_bounds")
                        acc[c] = jnp.where(mask, got, acc[c])
                for c in range(3):
                    picked[first + s, 4 * e + c : 4 * e + c + 1, :] = jnp.sum(acc[c], axis=0, keepdims=True)
                picked[first + s, q : q + 1, :] = blank

    def loop(i, carry):
        first = i * (DENSE + SPARSE)
        sparse(first)
        dense(first + SPARSE)
        return carry

    lax.fori_loop(0, senders // (DENSE + SPARSE), loop, 0)


def last_call(prov, xlo, xhi, source, fromlow, fromhigh, arrived):
    _, nx, ny, nz = prov.shape
    rows = source.shape[0]
    return pl.pallas_call(
        last_kernel,
        out_shape=(
            jax.ShapeDtypeStruct(prov.shape, F32),
            jax.ShapeDtypeStruct(arrived.shape, F32),
        ),
        in_specs=[pl.BlockSpec(memory_space=VMEM)] * 7,
        out_specs=(pl.BlockSpec(memory_space=VMEM),) * 2,
        scratch_shapes=[
            VMEM((rows, 32, nz), F32),
            VMEM((rows, 32, nz), F32),
            VMEM((384, 256), BF16),
        ],
        name="last",
    )(prov, xlo, xhi, source, fromlow, fromhigh, arrived)


def ring(value, axis, shift):
    count = lax.axis_size(axis)
    return lax.ppermute(value, axis, [(i, (i + shift) % count) for i in range(count)])


def body(velocity, marker_force, marker_cell, block_brick):
    devices = lax.axis_size("gx") * lax.axis_size("gy")
    blocks = marker_cell.shape[0]
    axes = ("gx", "gy")
    xlo = ring(velocity[:, -1], "gx", 1)
    xhi = ring(velocity[:, 0], "gx", -1)
    ylo = ring(velocity[:, :, -1], "gy", 1)
    yhi = ring(velocity[:, :, 0], "gy", -1)
    outgoing, target = pack(block_brick.reshape(blocks), marker_force, marker_cell, devices)
    arrived = lax.all_to_all(outgoing, axes, split_axis=0, concat_axis=0, tiled=True)
    prov, elo, ehi, spread = spread_call(arrived, velocity, xlo, xhi, ylo, yhi, 6)
    hlo, hhi = ring(ehi, "gx", 1), ring(elo, "gx", -1)
    source, tolow, tohigh = edges_call(prov, hlo, hhi)
    fromlow, fromhigh = ring(tohigh, "gy", 1), ring(tolow, "gy", -1)
    prov, elo, ehi = step_call(prov, hlo, hhi, source, fromlow, fromhigh, spread, 5)
    hlo, hhi = ring(ehi, "gx", 1), ring(elo, "gx", -1)
    source, tolow, tohigh = edges_call(prov, hlo, hhi)
    fromlow, fromhigh = ring(tohigh, "gy", 1), ring(tolow, "gy", -1)
    final, picked = last_call(prov, hlo, hhi, source, fromlow, fromhigh, arrived)
    back = lax.all_to_all(picked, axes, split_axis=0, concat_axis=0, tiled=True)
    return final, unpack(target, back, blocks)


def solution(mesh):
    return jax.shard_map(
        body,
        mesh=mesh,
        in_specs=(
            P(None, "gx", "gy", None),
            P(None, ("gx", "gy"), None),
            P(("gx", "gy"), None),
            P(("gx", "gy"), None),
        ),
        out_specs=(P(None, "gx", "gy", None), P(None, ("gx", "gy"), None)),
        check_vma=False,
    )
```

```python
import functools

import jax
import jax.numpy as jnp
from jax import lax
from jax.experimental import pallas as pl
from jax.experimental.pallas import tpu as pltpu
from jax.sharding import PartitionSpec as P


F32 = jnp.float32
BF16 = jnp.bfloat16
VMEM = pltpu.VMEM
SMEM = pltpu.SMEM


def pack_kernel(bb_any, force_any, cell_any, out, tgt, bb, force, cell, cnt, comb, sems):
    devices = out.shape[0]
    blocks = force.shape[1]
    copies = [
        pltpu.make_async_copy(src, dst, sems.at[i])
        for i, (src, dst) in enumerate(((bb_any, bb), (force_any, force), (cell_any, cell)))
    ]
    for copy in copies:
        copy.start()
    sub = lax.broadcasted_iota(jnp.int32, out.shape, 1)
    out[...] = jnp.where(sub % 4 == 3, -1.0, 0.0)

    def clear(i, carry):
        cnt[i] = 0
        return carry

    lax.fori_loop(0, devices, clear, 0, unroll=8)
    copies[0].wait()

    def slots(k, carry):
        for i in range(8):
            d = bb[8 * k + i]
            e = cnt[d]
            cnt[d] = e + 1
            tgt[8 * k + i] = 2 * d + e
        return carry

    lax.fori_loop(0, blocks // 8, slots, 0)
    copies[1].wait()
    copies[2].wait()
    for k in range(0, blocks, 8):
        for c in range(3):
            comb[pl.ds(8 * k + c, 8, 8), :] = force[c, k : k + 8, :]
        comb[pl.ds(8 * k + 3, 8, 8), :] = cell[k : k + 8, :].astype(F32)

    def eight(k, carry):
        first = pl.multiple_of(8 * k, 8)
        where = [tgt[first + i] for i in range(8)]
        rows = [comb[pl.ds(pl.multiple_of(8 * (first + i), 8), 4), :] for i in range(8)]
        for t, value in zip(where, rows):
            out[t >> 1, pl.ds(4 * (t & 1), 4), :] = value
        return carry

    lax.fori_loop(0, blocks // 8, eight, 0)


def pack(block_brick, force, cell, devices):
    blocks, width = cell.shape
    return pl.pallas_call(
        pack_kernel,
        out_shape=(
            jax.ShapeDtypeStruct((devices, 8, width), F32),
            jax.ShapeDtypeStruct((blocks,), jnp.int32),
        ),
        in_specs=[pl.BlockSpec(memory_space=pl.ANY)] * 3,
        out_specs=(pl.BlockSpec(memory_space=VMEM), pl.BlockSpec(memory_space=SMEM)),
        scratch_shapes=[
            SMEM((blocks,), jnp.int32),
            VMEM(force.shape, F32),
            VMEM(cell.shape, jnp.int32),
            SMEM((devices,), jnp.int32),
            VMEM((8 * blocks, width), F32),
            pltpu.SemaphoreType.DMA((3,)),
        ],
        name="pack",
    )(block_brick, force, cell)


def unpack_kernel(tgt, back, out, comb):
    blocks = out.shape[1]

    def eight(k, carry):
        first = pl.multiple_of(8 * k, 8)
        rows = []
        for i in range(8):
            t = tgt[first + i]
            rows.append(back[t >> 1, pl.ds(4 * (t & 1), 4), :])
        for i in range(8):
            comb[pl.ds(pl.multiple_of(8 * (first + i), 8), 4), :] = rows[i]
        return carry

    lax.fori_loop(0, blocks // 8, eight, 0)
    for k in range(0, blocks, 8):
        for c in range(3):
            out[c, k : k + 8, :] = comb[pl.ds(8 * k + c, 8, 8), :]


def unpack(tgt, back, blocks):
    return pl.pallas_call(
        unpack_kernel,
        out_shape=jax.ShapeDtypeStruct((3, blocks, back.shape[2]), F32),
        in_specs=[pl.BlockSpec(memory_space=SMEM), pl.BlockSpec(memory_space=VMEM)],
        out_specs=pl.BlockSpec(memory_space=VMEM),
        scratch_shapes=[VMEM((8 * blocks, back.shape[2]), F32)],
        compiler_params=pltpu.CompilerParams(vmem_limit_bytes=6 << 20),
        name="unpack",
    )(tgt, back)


def zshift(v, lane):
    size = v.shape[-1]
    up = jnp.where(lane == size - 1, 0.0, pltpu.roll(v, size - 1, v.ndim - 1))
    down = jnp.where(lane == 0, 0.0, pltpu.roll(v, 1, v.ndim - 1))
    return up, down


def edge_flags():
    gx, gy = lax.axis_index("gx"), lax.axis_index("gy")
    nx, ny = lax.axis_size("gx"), lax.axis_size("gy")
    return gx > 0, gx < nx - 1, gy > 0, gy < ny - 1


def divergence(p, nx, source, tolow, tohigh, comps):
    depth = tolow.shape[0] - len(comps) - 1
    lane = lax.broadcasted_iota(jnp.int32, (16, 128), 1)
    sub = lax.broadcasted_iota(jnp.int32, (16, 128), 0)
    low_edges = jnp.zeros((16, 128), F32)
    high_edges = jnp.zeros((16, 128), F32)
    for x in range(nx):
        p1 = p(1, x)
        ym = jnp.where(sub == 0, 0.0, pltpu.roll(p1, 1, 0))
        yp = jnp.where(sub == 15, 0.0, pltpu.roll(p1, 15, 0))
        up, down = zshift(p(2, x), lane)
        value = (yp - ym) + (up - down)
        if x < nx - 1:
            value = value + p(0, x + 1)
        if x > 0:
            value = value - p(0, x - 1)
        source[x] = value
        first, last = jnp.broadcast_to(p1[0:1], (16, 128)), jnp.broadcast_to(p1[15:16], (16, 128))
        if x < depth:
            tolow[x] = value
            low_edges = jnp.where(sub == 2 * x, first, jnp.where(sub == 2 * x + 1, last, low_edges))
        k = x - (nx - depth)
        if k >= 0:
            tohigh[k] = value
            high_edges = jnp.where(sub == 2 * k, first, jnp.where(sub == 2 * k + 1, last, high_edges))
    for i, c in enumerate(comps):
        tolow[depth + i] = p(c, 0)
        tohigh[depth + i] = p(c, nx - 1)
    tolow[depth + len(comps)] = low_edges
    tohigh[depth + len(comps)] = high_edges


ALL = (0, 1, 2)
HALO1, HALO2 = 5, 4
CHUNK = 16


def split(v):
    hi = v.astype(BF16)
    lo = (v - hi.astype(F32)).astype(BF16)
    return hi, lo


def one_hots(packet, iota_r, iota_c):
    number = packet.astype(jnp.int32)
    row = ((number >> 13) * 128 + (number & 127)).astype(F32)
    col = ((number >> 7) & 63).astype(F32)
    hi = packet.astype(BF16).astype(F32)
    lo = packet - hi
    one, zero = jnp.ones((), BF16), jnp.zeros((), BF16)
    out = []
    for e in range(2):
        q = 4 * e + 3
        rr = jnp.broadcast_to(row[q : q + 1], (256, 128)).astype(BF16)
        hot = jnp.where(iota_r == rr, one, zero)
        cc = jnp.broadcast_to(col[q : q + 1], (64, 128)).astype(BF16)
        mask = iota_c == cc
        rows = []
        for c in range(3):
            p = 4 * e + c
            for src in (hi, lo):
                val = jnp.broadcast_to(src[p : p + 1], (64, 128)).astype(BF16)
                rows.append(jnp.where(mask, val, zero))
        rows.append(jnp.where(mask, one, zero))
        out.append((hot, jnp.concatenate(rows, axis=0)))
    return out


def spread_kernel(arrived, vel, xlo, xhi, ylo, yhi, prov, spread, source, tolow, tohigh, acc):
    senders = arrived.shape[0]
    iota_r = lax.broadcasted_iota(jnp.int32, (256, 128), 0).astype(F32).astype(BF16)
    iota_c = lax.broadcasted_iota(jnp.int32, (64, 128), 0).astype(F32).astype(BF16)
    dims = (((1,), (1,)), ((), ()))
    acc[...] = jnp.zeros_like(acc)

    def loop(i, carry):
        hots, vals = [], []
        for s in range(CHUNK):
            for hot, val in one_hots(arrived[i * CHUNK + s], iota_r, iota_c):
                hots.append(hot)
                vals.append(val)
        acc[...] += lax.dot_general(
            jnp.concatenate(vals, axis=1), jnp.concatenate(hots, axis=1), dims, preferred_element_type=F32
        )
        return carry

    lax.fori_loop(0, senders // CHUNK, loop, 0)
    for c in range(3):
        total = acc[128 * c : 128 * c + 64] + acc[128 * c + 64 : 128 * c + 128]
        spread[c, 0:4] = total[:, :128].reshape(4, 16, 128)
        spread[c, 4:8] = total[:, 128:].reshape(4, 16, 128)
    spread[3, 0:4] = acc[384:448, :128].reshape(4, 16, 128)
    spread[3, 4:8] = acc[384:448, 128:].reshape(4, 16, 128)
    has_xlo, has_xhi, has_ylo, has_yhi = edge_flags()
    lane = lax.broadcasted_iota(jnp.int32, (16, 128), 1)
    sub = lax.broadcasted_iota(jnp.int32, (16, 128), 0)
    nx = vel.shape[1]
    for c in range(3):
        for x in range(nx):
            here = vel[c, x]
            before = vel[c, x - 1] if x else jnp.where(has_xlo, xlo[c], 0.0)
            after = vel[c, x + 1] if x < nx - 1 else jnp.where(has_xhi, xhi[c], 0.0)
            left = jnp.broadcast_to(jnp.where(has_ylo, ylo[c, x : x + 1], 0.0), (16, 128))
            right = jnp.broadcast_to(jnp.where(has_yhi, yhi[c, x : x + 1], 0.0), (16, 128))
            ym = jnp.where(sub == 0, left, pltpu.roll(here, 1, 0))
            yp = jnp.where(sub == 15, right, pltpu.roll(here, 15, 0))
            up, down = zshift(here, lane)
            total = ((after + before) + (yp + ym)) + (up + down)
            value = here + 0.5 * (0.2 * (total - 6.0 * here) + spread[c, x])
            prov[c, x] = value
    divergence(lambda c, x: prov[c, x], nx, source, tolow, tohigh, ALL)


def spread_call(arrived, vel, xlo, xhi, ylo, yhi):
    _, nx, ny, nz = vel.shape
    return pl.pallas_call(
        spread_kernel,
        out_shape=(
            jax.ShapeDtypeStruct(vel.shape, F32),
            jax.ShapeDtypeStruct((4, nx, ny, nz), F32),
            jax.ShapeDtypeStruct((nx, ny, nz), F32),
            jax.ShapeDtypeStruct((HALO1 + 4, ny, nz), F32),
            jax.ShapeDtypeStruct((HALO1 + 4, ny, nz), F32),
        ),
        in_specs=[pl.BlockSpec(memory_space=VMEM)] * 6,
        out_specs=(pl.BlockSpec(memory_space=VMEM),) * 5,
        scratch_shapes=[VMEM((448, 256), F32)],
        compiler_params=pltpu.CompilerParams(vmem_limit_bytes=28 << 20),
        name="spread",
    )(arrived, vel, xlo, xhi, ylo, yhi)


def edges_kernel(comps, prov, brick, xlo, xhi, source, tolow, tohigh):
    nx = brick.shape[0]
    rows = source.shape[0]
    halo = (rows - nx) // 2
    has_xlo, has_xhi, _, _ = edge_flags()
    sub8 = lax.broadcasted_iota(jnp.int32, (8, 128), 0)
    zero8 = jnp.zeros((8, 128), F32)
    low_edge, high_edge = xlo[halo + len(comps)], xhi[halo + len(comps)]
    for j in range(rows):
        x = j - halo
        if x < 0:
            value = xlo[j]
            if x == -1:
                value = value + prov[0, 0]
        elif x < nx:
            value = brick[x]
            if x == 0:
                value = value - jnp.where(has_xlo, xlo[halo], 0.0)
            if x == nx - 1:
                value = value + jnp.where(has_xhi, xhi[halo], 0.0)
        else:
            value = xhi[x - nx]
            if x == nx:
                value = value - prov[0, nx - 1]
        source[j] = value
        high, low = value[8:16], value[0:8]
        if 0 <= x < nx:
            for c in comps if 1 in comps else (1,):
                p = prov[c, x]
                high = jnp.where(sub8 == c, pltpu.roll(p[8:16], c + 1, 0), high)
                low = jnp.where(sub8 == 5 + c, pltpu.roll(p[0:8], 5 + c, 0), low)
        else:
            first, last = edge_rows(low_edge if x < 0 else high_edge, j if x < 0 else x - nx)
            high = jnp.where(sub8 == 1, jnp.broadcast_to(last, (8, 128)), high)
            low = jnp.where(sub8 == 6, jnp.broadcast_to(first, (8, 128)), low)
            if 1 in comps and x in (-1, nx):
                packet = xlo if x < 0 else xhi
                for c in (0, 2):
                    p = packet[halo + c]
                    high = jnp.where(sub8 == c, pltpu.roll(p[8:16], c + 1, 0), high)
                    low = jnp.where(sub8 == 5 + c, pltpu.roll(p[0:8], 5 + c, 0), low)
        tohigh[j] = high
        tolow[j] = low


def edge_rows(edges, k):
    return edges[2 * k : 2 * k + 1], edges[2 * k + 1 : 2 * k + 2]


def edges_call(prov, brick, xlo, xhi, comps):
    nx, ny, nz = brick.shape
    rows = nx + 2 * (xlo.shape[0] - len(comps) - 1)
    return pl.pallas_call(
        functools.partial(edges_kernel, comps),
        out_shape=(
            jax.ShapeDtypeStruct((rows, ny, nz), F32),
            jax.ShapeDtypeStruct((rows, 8, nz), F32),
            jax.ShapeDtypeStruct((rows, 8, nz), F32),
        ),
        in_specs=[pl.BlockSpec(memory_space=VMEM)] * 4,
        out_specs=(pl.BlockSpec(memory_space=VMEM),) * 3,
        compiler_params=pltpu.CompilerParams(vmem_limit_bytes=6 << 20),
        name="edges",
    )(prov, brick, xlo, xhi)


def solve(prov, xlo, xhi, source, fromlow, fromhigh, pa, pb):
    rows = source.shape[0]
    nx = prov.shape[1]
    halo = (rows - nx) // 2
    low_edge, high_edge = xlo[xlo.shape[0] - 1], xhi[xhi.shape[0] - 1]
    has_xlo, has_xhi, has_ylo, has_yhi = edge_flags()
    sub = lax.broadcasted_iota(jnp.int32, (32, 128), 0)
    lane = lax.broadcasted_iota(jnp.int32, (32, 128), 1)
    inside = ((sub >= 8) | has_ylo) & ((sub < 24) | has_yhi)

    def masked(v, j):
        keep = inside
        if j < halo:
            keep = inside & has_xlo
        elif j >= halo + nx:
            keep = inside & has_xhi
        return jnp.where(keep, v, 0.0)

    src = []
    for j in range(rows):
        lowp = fromlow[j]
        highp = fromhigh[j]
        x = j - halo
        if 0 <= x < nx:
            first, last = prov[1, x, 0:1], prov[1, x, 15:16]
        else:
            first, last = edge_rows(low_edge if x < 0 else high_edge, j if x < 0 else x - nx)
        low1 = jnp.where(has_ylo, lowp[1:2], 0.0)
        high1 = jnp.where(has_yhi, highp[6:7], 0.0)
        value = jnp.concatenate([lowp, source[j], highp], axis=0)
        add = jnp.where(sub == 7, jnp.broadcast_to(first, (32, 128)), 0.0)
        add = jnp.where(sub == 8, jnp.broadcast_to(-low1, (32, 128)), add)
        add = jnp.where(sub == 23, jnp.broadcast_to(high1, (32, 128)), add)
        add = jnp.where(sub == 24, jnp.broadcast_to(-last, (32, 128)), add)
        value = masked((value + add) * (1.0 / 6.0), j)
        src.append(value)
        pa[j] = -value
    cur, new = pa, pb
    for sweep in range(1, 4):
        for j in range(sweep, rows - sweep):
            here = cur[j]
            up, down = zshift(here, lane)
            total = (cur[j - 1] + cur[j + 1]) + (pltpu.roll(here, 1, 0) + pltpu.roll(here, 31, 0))
            total = total + (up + down)
            new[j] = masked(total * (1.0 / 6.0) - src[j], j)
        cur, new = new, cur
    return cur, halo


def step_kernel(prov, xlo, xhi, source, fromlow, fromhigh, spread, prov2, source2, tolow, tohigh, pa, pb, ux):
    nx = prov.shape[1]
    p, halo = solve(prov, xlo, xhi, source, fromlow, fromhigh, pa, pb)
    has_xlo, has_xhi, has_ylo, has_yhi = edge_flags()
    sub = lax.broadcasted_iota(jnp.int32, (32, 128), 0)
    lane = lax.broadcasted_iota(jnp.int32, (32, 128), 1)
    inside = ((sub >= 8) | has_ylo) & ((sub < 24) | has_yhi)
    for x in range(-1, nx + 1):
        j = x + halo
        here = p[j]
        up, down = zshift(here, lane)
        slopes = (
            p[j + 1] - p[j - 1],
            pltpu.roll(here, 31, 0) - pltpu.roll(here, 1, 0),
            up - down,
        )
        keep = inside
        if x < 0:
            keep = inside & has_xlo
        elif x >= nx:
            keep = inside & has_xhi
        lowp, highp = fromlow[j], fromhigh[j]
        for c in range(3):
            mid = xlo[halo + c] if x < 0 else xhi[halo + c] if x >= nx else prov[c, x]
            wide = jnp.concatenate(
                [pltpu.roll(lowp, 7 - c, 0), mid, pltpu.roll(highp, 3 - c, 0)], axis=0
            )
            ux[c, x + 1] = jnp.where(keep, wide - 0.25 * slopes[c], 0.0)
    lane16 = lax.broadcasted_iota(jnp.int32, (16, 128), 1)
    for c in range(3):
        for x in range(nx):
            here = ux[c, x + 1]
            ys = pltpu.roll(here, 1, 0) + pltpu.roll(here, 31, 0)
            mid = here[8:24]
            up, down = zshift(mid, lane16)
            total = (ux[c, x, 8:24] + ux[c, x + 2, 8:24]) + ys[8:24] + (up + down)
            pull = spread[c, x] - spread[3, x] * mid
            value = mid + 0.5 * (0.2 * (total - 6.0 * mid) + pull)
            prov2[c, x] = value
    divergence(lambda c, x: prov2[c, x], nx, source2, tolow, tohigh, (0,))


def step_call(prov, xlo, xhi, source, fromlow, fromhigh, spread):
    _, nx, ny, nz = prov.shape
    rows = source.shape[0]
    return pl.pallas_call(
        step_kernel,
        out_shape=(
            jax.ShapeDtypeStruct(prov.shape, F32),
            jax.ShapeDtypeStruct((nx, ny, nz), F32),
            jax.ShapeDtypeStruct((HALO2 + 2, ny, nz), F32),
            jax.ShapeDtypeStruct((HALO2 + 2, ny, nz), F32),
        ),
        in_specs=[pl.BlockSpec(memory_space=VMEM)] * 7,
        out_specs=(pl.BlockSpec(memory_space=VMEM),) * 4,
        scratch_shapes=[
            VMEM((rows, 32, nz), F32),
            VMEM((rows, 32, nz), F32),
            VMEM((3, nx + 2, 32, nz), F32),
        ],
        compiler_params=pltpu.CompilerParams(vmem_limit_bytes=12 << 20),
        name="step",
    )(prov, xlo, xhi, source, fromlow, fromhigh, spread)


DENSE, SPARSE = 11, 5


def last_kernel(prov, xlo, xhi, source, fromlow, fromhigh, arrived, vel, picked, pa, pb, table):
    nx = prov.shape[1]
    senders = arrived.shape[0]
    p, halo = solve(prov, xlo, xhi, source, fromlow, fromhigh, pa, pb)
    lane16 = lax.broadcasted_iota(jnp.int32, (16, 128), 1)
    for x in range(nx):
        j = x + halo
        here = p[j]
        mid = here[8:24]
        up, down = zshift(mid, lane16)
        slopes = (
            p[j + 1, 8:24] - p[j - 1, 8:24],
            (pltpu.roll(here, 31, 0) - pltpu.roll(here, 1, 0))[8:24],
            up - down,
        )
        for c in range(3):
            value = prov[c, x] - 0.25 * slopes[c]
            vel[c, x] = value
            hi, lo = split(value)
            r = 64 * c + 16 * (x % 4)
            k = 128 * (x // 4)
            table[r : r + 16, k : k + 128] = hi
            table[192 + r : 192 + r + 16, k : k + 128] = lo
    rows8 = lax.broadcasted_iota(jnp.int32, (8, 128), 0)
    iota_r = lax.broadcasted_iota(jnp.int32, (256, 128), 0).astype(F32).astype(BF16)
    iota_c = lax.broadcasted_iota(jnp.int32, (64, 128), 0)
    one, zero = jnp.ones((), BF16), jnp.zeros((), BF16)
    blank = jnp.zeros((1, 128), F32)

    def dense(first):
        hot, cols = [], []
        for s in range(DENSE):
            number = arrived[first + s].astype(jnp.int32)
            rowf = ((number >> 13) * 128 + (number & 127)).astype(F32)
            col = (number >> 7) & 63
            for e in range(2):
                q = 4 * e + 3
                rr = jnp.broadcast_to(rowf[q : q + 1], (256, 128)).astype(BF16)
                hot.append(jnp.where(iota_r == rr, one, zero))
                cols.append(col[q : q + 1])
        got = jnp.dot(table[...], jnp.concatenate(hot, axis=1), preferred_element_type=F32)
        for s in range(DENSE):
            for e in range(2):
                k = 128 * (2 * s + e)
                mask = iota_c == jnp.broadcast_to(cols[2 * s + e], (64, 128))
                for c in range(3):
                    val = got[64 * c : 64 * c + 64, k : k + 128] + got[192 + 64 * c : 256 + 64 * c, k : k + 128]
                    val = jnp.where(mask, val, 0.0)
                    picked[first + s, 4 * e + c : 4 * e + c + 1, :] = jnp.sum(val, axis=0, keepdims=True)
                picked[first + s, 4 * e + 3 : 4 * e + 4, :] = blank

    def sparse(first):
        for s in range(SPARSE):
            number = arrived[first + s].astype(jnp.int32)
            for e in range(2):
                q = 4 * e + 3
                cell = jnp.broadcast_to(number[q : q + 1], (8, 128))
                z = cell & 127
                column = (cell >> 7) - rows8
                acc = [jnp.zeros((8, 128), F32) for _ in range(3)]
                for g in range(2 * nx):
                    mask = column == 8 * g
                    for c in range(3):
                        field = vel[c, g // 2, 8 * (g % 2) : 8 * (g % 2) + 8, :]
                        got = jnp.take_along_axis(field, z, axis=1, mode="promise_in_bounds")
                        acc[c] = jnp.where(mask, got, acc[c])
                for c in range(3):
                    picked[first + s, 4 * e + c : 4 * e + c + 1, :] = jnp.sum(acc[c], axis=0, keepdims=True)
                picked[first + s, q : q + 1, :] = blank

    def loop(i, carry):
        first = i * (DENSE + SPARSE)
        sparse(first)
        dense(first + SPARSE)
        return carry

    lax.fori_loop(0, senders // (DENSE + SPARSE), loop, 0)


def last_call(prov, xlo, xhi, source, fromlow, fromhigh, arrived):
    _, nx, ny, nz = prov.shape
    rows = source.shape[0]
    return pl.pallas_call(
        last_kernel,
        out_shape=(
            jax.ShapeDtypeStruct(prov.shape, F32),
            jax.ShapeDtypeStruct(arrived.shape, F32),
        ),
        in_specs=[pl.BlockSpec(memory_space=VMEM)] * 7,
        out_specs=(pl.BlockSpec(memory_space=VMEM),) * 2,
        scratch_shapes=[
            VMEM((rows, 32, nz), F32),
            VMEM((rows, 32, nz), F32),
            VMEM((384, 256), BF16),
        ],
        compiler_params=pltpu.CompilerParams(vmem_limit_bytes=28 << 20),
        name="last",
    )(prov, xlo, xhi, source, fromlow, fromhigh, arrived)


def ring(value, axis, shift):
    count = lax.axis_size(axis)
    return lax.ppermute(value, axis, [(i, (i + shift) % count) for i in range(count)])


def body(velocity, marker_force, marker_cell, block_brick):
    devices = lax.axis_size("gx") * lax.axis_size("gy")
    blocks = marker_cell.shape[0]
    axes = ("gx", "gy")
    xlo = ring(velocity[:, -1], "gx", 1)
    xhi = ring(velocity[:, 0], "gx", -1)
    ylo = ring(velocity[:, :, -1], "gy", 1)
    yhi = ring(velocity[:, :, 0], "gy", -1)
    outgoing, target = pack(block_brick.reshape(blocks), marker_force, marker_cell, devices)
    arrived = lax.all_to_all(outgoing, axes, split_axis=0, concat_axis=0, tiled=True)
    prov, spread, brick, tolow, tohigh = spread_call(arrived, velocity, xlo, xhi, ylo, yhi)
    xlo, xhi = ring(tohigh, "gx", 1), ring(tolow, "gx", -1)
    source, tolow, tohigh = edges_call(prov, brick, xlo, xhi, ALL)
    fromlow, fromhigh = ring(tohigh, "gy", 1), ring(tolow, "gy", -1)
    prov, brick, tolow, tohigh = step_call(prov, xlo, xhi, source, fromlow, fromhigh, spread)
    xlo, xhi = ring(tohigh, "gx", 1), ring(tolow, "gx", -1)
    source, tolow, tohigh = edges_call(prov, brick, xlo, xhi, (0,))
    fromlow, fromhigh = ring(tohigh, "gy", 1), ring(tolow, "gy", -1)
    final, picked = last_call(prov, xlo, xhi, source, fromlow, fromhigh, arrived)
    back = lax.all_to_all(picked, axes, split_axis=0, concat_axis=0, tiled=True)
    return final, unpack(target, back, blocks)


def solution(mesh):
    return jax.shard_map(
        body,
        mesh=mesh,
        in_specs=(
            P(None, "gx", "gy", None),
            P(None, ("gx", "gy"), None),
            P(("gx", "gy"), None),
            P(("gx", "gy"), None),
        ),
        out_specs=(P(None, "gx", "gy", None), P(None, ("gx", "gy"), None)),
        check_vma=False,
    )
```

```python
import functools

import jax
import jax.numpy as jnp
from jax import lax
from jax.experimental import pallas as pl
from jax.experimental.pallas import tpu as pltpu
from jax.sharding import PartitionSpec as P


F32 = jnp.float32
BF16 = jnp.bfloat16
VMEM = pltpu.VMEM
SMEM = pltpu.SMEM


def pack_kernel(bb_any, force_any, cell_any, out, tgt, bb, force, cell, cnt, comb, sems):
    devices = out.shape[0]
    blocks = force.shape[1]
    copies = [
        pltpu.make_async_copy(src, dst, sems.at[i])
        for i, (src, dst) in enumerate(((bb_any, bb), (force_any, force), (cell_any, cell)))
    ]
    for copy in copies:
        copy.start()
    sub = lax.broadcasted_iota(jnp.int32, out.shape, 1)
    out[...] = jnp.where(sub % 4 == 3, -1.0, 0.0)

    def clear(i, carry):
        cnt[i] = 0
        return carry

    lax.fori_loop(0, devices, clear, 0, unroll=8)
    copies[0].wait()

    def slots(k, carry):
        for i in range(8):
            d = bb[8 * k + i]
            e = cnt[d]
            cnt[d] = e + 1
            tgt[8 * k + i] = 2 * d + e
        return carry

    lax.fori_loop(0, blocks // 8, slots, 0)
    copies[1].wait()
    copies[2].wait()
    for k in range(0, blocks, 8):
        for c in range(3):
            comb[pl.ds(8 * k + c, 8, 8), :] = force[c, k : k + 8, :]
        comb[pl.ds(8 * k + 3, 8, 8), :] = cell[k : k + 8, :].astype(F32)

    def eight(k, carry):
        first = pl.multiple_of(8 * k, 8)
        where = [tgt[first + i] for i in range(8)]
        rows = [comb[pl.ds(pl.multiple_of(8 * (first + i), 8), 4), :] for i in range(8)]
        for t, value in zip(where, rows):
            out[t >> 1, pl.ds(4 * (t & 1), 4), :] = value
        return carry

    lax.fori_loop(0, blocks // 8, eight, 0)


def pack(block_brick, force, cell, devices):
    blocks, width = cell.shape
    return pl.pallas_call(
        pack_kernel,
        out_shape=(
            jax.ShapeDtypeStruct((devices, 8, width), F32),
            jax.ShapeDtypeStruct((blocks,), jnp.int32),
        ),
        in_specs=[pl.BlockSpec(memory_space=pl.ANY)] * 3,
        out_specs=(pl.BlockSpec(memory_space=VMEM), pl.BlockSpec(memory_space=SMEM)),
        scratch_shapes=[
            SMEM((blocks,), jnp.int32),
            VMEM(force.shape, F32),
            VMEM(cell.shape, jnp.int32),
            SMEM((devices,), jnp.int32),
            VMEM((8 * blocks, width), F32),
            pltpu.SemaphoreType.DMA((3,)),
        ],
        name="pack",
    )(block_brick, force, cell)


def unpack_kernel(tgt, back, out):
    blocks, width = out.shape[1:]

    def eight(k, carry):
        first = pl.multiple_of(8 * k, 8)
        rows = []
        for i in range(8):
            t = tgt[first + i]
            base = pl.multiple_of((t & 1) * 3 * width, 128)
            rows.append([back[t >> 1, :, pl.ds(base + c * width, width)] for c in range(3)])
        for c in range(3):
            for i in range(8):
                out[c, pl.ds(first + i, 1), :] = rows[i][c]
        return carry

    lax.fori_loop(0, blocks // 8, eight, 0)


def unpack(tgt, back, blocks):
    return pl.pallas_call(
        unpack_kernel,
        out_shape=jax.ShapeDtypeStruct((3, blocks, back.shape[2] // 6), F32),
        in_specs=[pl.BlockSpec(memory_space=SMEM), pl.BlockSpec(memory_space=VMEM)],
        out_specs=pl.BlockSpec(memory_space=VMEM),
        compiler_params=pltpu.CompilerParams(vmem_limit_bytes=6 << 20),
        name="unpack",
    )(tgt, back)


def zshift(v, lane):
    size = v.shape[-1]
    up = jnp.where(lane == size - 1, 0.0, pltpu.roll(v, size - 1, v.ndim - 1))
    down = jnp.where(lane == 0, 0.0, pltpu.roll(v, 1, v.ndim - 1))
    return up, down


def edge_flags():
    gx, gy = lax.axis_index("gx"), lax.axis_index("gy")
    nx, ny = lax.axis_size("gx"), lax.axis_size("gy")
    return gx > 0, gx < nx - 1, gy > 0, gy < ny - 1


def is_even(axis):
    return lax.axis_index(axis) % 2 == 0


def place(low, high, first, second, axis):
    even = is_even(axis)
    first[...] = jnp.where(even, high[...], low[...])
    second[...] = jnp.where(even, low[...], high[...])


def pick(first, second, low, high, axis):
    even = is_even(axis)
    low[...] = jnp.where(even, second[...], first[...])
    high[...] = jnp.where(even, first[...], second[...])


def divergence(p, nx, source, tolow, tohigh, comps):
    depth = tolow.shape[0] - len(comps) - 1
    lane = lax.broadcasted_iota(jnp.int32, (16, 128), 1)
    sub = lax.broadcasted_iota(jnp.int32, (16, 128), 0)
    low_edges = jnp.zeros((16, 128), F32)
    high_edges = jnp.zeros((16, 128), F32)
    for x in range(nx):
        p1 = p(1, x)
        ym = jnp.where(sub == 0, 0.0, pltpu.roll(p1, 1, 0))
        yp = jnp.where(sub == 15, 0.0, pltpu.roll(p1, 15, 0))
        up, down = zshift(p(2, x), lane)
        value = (yp - ym) + (up - down)
        if x < nx - 1:
            value = value + p(0, x + 1)
        if x > 0:
            value = value - p(0, x - 1)
        source[x] = value
        first, last = jnp.broadcast_to(p1[0:1], (16, 128)), jnp.broadcast_to(p1[15:16], (16, 128))
        if x < depth:
            tolow[x] = value
            low_edges = jnp.where(sub == 2 * x, first, jnp.where(sub == 2 * x + 1, last, low_edges))
        k = x - (nx - depth)
        if k >= 0:
            tohigh[k] = value
            high_edges = jnp.where(sub == 2 * k, first, jnp.where(sub == 2 * k + 1, last, high_edges))
    for i, c in enumerate(comps):
        tolow[depth + i] = p(c, 0)
        tohigh[depth + i] = p(c, nx - 1)
    tolow[depth + len(comps)] = low_edges
    tohigh[depth + len(comps)] = high_edges


ALL = (0, 1, 2)
HALO1, HALO2 = 5, 4
CHUNK = 16


def split(v):
    hi = v.astype(BF16)
    lo = (v - hi.astype(F32)).astype(BF16)
    return hi, lo


def one_hots(packet, iota_r, iota_c):
    number = packet.astype(jnp.int32)
    row = ((number >> 13) * 128 + (number & 127)).astype(F32)
    col = ((number >> 7) & 63).astype(F32)
    hi = packet.astype(BF16).astype(F32)
    lo = packet - hi
    one, zero = jnp.ones((), BF16), jnp.zeros((), BF16)
    out = []
    for e in range(2):
        q = 4 * e + 3
        rr = jnp.broadcast_to(row[q : q + 1], (256, 128)).astype(BF16)
        hot = jnp.where(iota_r == rr, one, zero)
        cc = jnp.broadcast_to(col[q : q + 1], (64, 128)).astype(BF16)
        mask = iota_c == cc
        rows = []
        for c in range(3):
            p = 4 * e + c
            for src in (hi, lo):
                val = jnp.broadcast_to(src[p : p + 1], (64, 128)).astype(BF16)
                rows.append(jnp.where(mask, val, zero))
        rows.append(jnp.where(mask, one, zero))
        out.append((hot, jnp.concatenate(rows, axis=0)))
    return out


def spread_kernel(arrived, vel, x1, x2, y1, y2, prov, spread, source, out1, out2, acc, xlo, xhi, ylo, yhi, tolow, tohigh):
    pick(x1, x2, xlo, xhi, "gx")
    pick(y1, y2, ylo, yhi, "gy")
    senders = arrived.shape[0]
    iota_r = lax.broadcasted_iota(jnp.int32, (256, 128), 0).astype(F32).astype(BF16)
    iota_c = lax.broadcasted_iota(jnp.int32, (64, 128), 0).astype(F32).astype(BF16)
    dims = (((1,), (1,)), ((), ()))
    acc[...] = jnp.zeros_like(acc)

    def loop(i, carry):
        hots, vals = [], []
        for s in range(CHUNK):
            for hot, val in one_hots(arrived[i * CHUNK + s], iota_r, iota_c):
                hots.append(hot)
                vals.append(val)
        acc[...] += lax.dot_general(
            jnp.concatenate(vals, axis=1), jnp.concatenate(hots, axis=1), dims, preferred_element_type=F32
        )
        return carry

    lax.fori_loop(0, senders // CHUNK, loop, 0)
    for c in range(3):
        total = acc[128 * c : 128 * c + 64] + acc[128 * c + 64 : 128 * c + 128]
        spread[c, 0:4] = total[:, :128].reshape(4, 16, 128)
        spread[c, 4:8] = total[:, 128:].reshape(4, 16, 128)
    spread[3, 0:4] = acc[384:448, :128].reshape(4, 16, 128)
    spread[3, 4:8] = acc[384:448, 128:].reshape(4, 16, 128)
    has_xlo, has_xhi, has_ylo, has_yhi = edge_flags()
    lane = lax.broadcasted_iota(jnp.int32, (16, 128), 1)
    sub = lax.broadcasted_iota(jnp.int32, (16, 128), 0)
    nx = vel.shape[1]
    for c in range(3):
        for x in range(nx):
            here = vel[c, x]
            before = vel[c, x - 1] if x else jnp.where(has_xlo, xlo[c], 0.0)
            after = vel[c, x + 1] if x < nx - 1 else jnp.where(has_xhi, xhi[c], 0.0)
            left = jnp.broadcast_to(jnp.where(has_ylo, ylo[c, x : x + 1], 0.0), (16, 128))
            right = jnp.broadcast_to(jnp.where(has_yhi, yhi[c, x : x + 1], 0.0), (16, 128))
            ym = jnp.where(sub == 0, left, pltpu.roll(here, 1, 0))
            yp = jnp.where(sub == 15, right, pltpu.roll(here, 15, 0))
            up, down = zshift(here, lane)
            total = ((after + before) + (yp + ym)) + (up + down)
            value = here + 0.5 * (0.2 * (total - 6.0 * here) + spread[c, x])
            prov[c, x] = value
    divergence(lambda c, x: prov[c, x], nx, source, tolow, tohigh, ALL)
    place(tolow, tohigh, out1, out2, "gx")


def spread_call(arrived, vel, xlo, xhi, ylo, yhi):
    _, nx, ny, nz = vel.shape
    return pl.pallas_call(
        spread_kernel,
        out_shape=(
            jax.ShapeDtypeStruct(vel.shape, F32),
            jax.ShapeDtypeStruct((4, nx, ny, nz), F32),
            jax.ShapeDtypeStruct((nx, ny, nz), F32),
            jax.ShapeDtypeStruct((HALO1 + 4, ny, nz), F32),
            jax.ShapeDtypeStruct((HALO1 + 4, ny, nz), F32),
        ),
        in_specs=[pl.BlockSpec(memory_space=VMEM)] * 6,
        out_specs=(pl.BlockSpec(memory_space=VMEM),) * 5,
        scratch_shapes=[VMEM((448, 256), F32)]
        + [VMEM((3, ny, nz), F32)] * 2
        + [VMEM((3, nx, nz), F32)] * 2
        + [VMEM((HALO1 + 4, ny, nz), F32)] * 2,
        compiler_params=pltpu.CompilerParams(vmem_limit_bytes=28 << 20),
        name="spread",
    )(arrived, vel, xlo, xhi, ylo, yhi)


def edges_kernel(comps, prov, brick, x1, x2, source, out1, out2, xlo, xhi, tolow, tohigh):
    pick(x1, x2, xlo, xhi, "gx")
    nx = brick.shape[0]
    rows = source.shape[0]
    halo = (rows - nx) // 2
    has_xlo, has_xhi, _, _ = edge_flags()
    sub8 = lax.broadcasted_iota(jnp.int32, (8, 128), 0)
    zero8 = jnp.zeros((8, 128), F32)
    low_edge, high_edge = xlo[halo + len(comps)], xhi[halo + len(comps)]
    for j in range(rows):
        x = j - halo
        if x < 0:
            value = xlo[j]
            if x == -1:
                value = value + prov[0, 0]
        elif x < nx:
            value = brick[x]
            if x == 0:
                value = value - jnp.where(has_xlo, xlo[halo], 0.0)
            if x == nx - 1:
                value = value + jnp.where(has_xhi, xhi[halo], 0.0)
        else:
            value = xhi[x - nx]
            if x == nx:
                value = value - prov[0, nx - 1]
        source[j] = value
        high, low = value[8:16], value[0:8]
        if 0 <= x < nx:
            for c in comps if 1 in comps else (1,):
                p = prov[c, x]
                high = jnp.where(sub8 == c, pltpu.roll(p[8:16], c + 1, 0), high)
                low = jnp.where(sub8 == 5 + c, pltpu.roll(p[0:8], 5 + c, 0), low)
        else:
            first, last = edge_rows(low_edge if x < 0 else high_edge, j if x < 0 else x - nx)
            high = jnp.where(sub8 == 1, jnp.broadcast_to(last, (8, 128)), high)
            low = jnp.where(sub8 == 6, jnp.broadcast_to(first, (8, 128)), low)
            if 1 in comps and x in (-1, nx):
                packet = xlo if x < 0 else xhi
                for c in (0, 2):
                    p = packet[halo + c]
                    high = jnp.where(sub8 == c, pltpu.roll(p[8:16], c + 1, 0), high)
                    low = jnp.where(sub8 == 5 + c, pltpu.roll(p[0:8], 5 + c, 0), low)
        tohigh[j] = high
        tolow[j] = low
    place(tolow, tohigh, out1, out2, "gy")


def edge_rows(edges, k):
    return edges[2 * k : 2 * k + 1], edges[2 * k + 1 : 2 * k + 2]


def edges_call(prov, brick, xlo, xhi, comps):
    nx, ny, nz = brick.shape
    rows = nx + 2 * (xlo.shape[0] - len(comps) - 1)
    return pl.pallas_call(
        functools.partial(edges_kernel, comps),
        out_shape=(
            jax.ShapeDtypeStruct((rows, ny, nz), F32),
            jax.ShapeDtypeStruct((rows, 8, nz), F32),
            jax.ShapeDtypeStruct((rows, 8, nz), F32),
        ),
        in_specs=[pl.BlockSpec(memory_space=VMEM)] * 4,
        out_specs=(pl.BlockSpec(memory_space=VMEM),) * 3,
        scratch_shapes=[VMEM(xlo.shape, F32)] * 2 + [VMEM((rows, 8, nz), F32)] * 2,
        compiler_params=pltpu.CompilerParams(vmem_limit_bytes=6 << 20),
        name="edges",
    )(prov, brick, xlo, xhi)


def solve(prov, xlo, xhi, source, fromlow, fromhigh, pa, pb):
    rows = source.shape[0]
    nx = prov.shape[1]
    halo = (rows - nx) // 2
    low_edge, high_edge = xlo[xlo.shape[0] - 1], xhi[xhi.shape[0] - 1]
    has_xlo, has_xhi, has_ylo, has_yhi = edge_flags()
    sub = lax.broadcasted_iota(jnp.int32, (32, 128), 0)
    lane = lax.broadcasted_iota(jnp.int32, (32, 128), 1)
    inside = ((sub >= 8) | has_ylo) & ((sub < 24) | has_yhi)

    def masked(v, j):
        keep = inside
        if j < halo:
            keep = inside & has_xlo
        elif j >= halo + nx:
            keep = inside & has_xhi
        return jnp.where(keep, v, 0.0)

    src = []
    for j in range(rows):
        lowp = fromlow[j]
        highp = fromhigh[j]
        x = j - halo
        if 0 <= x < nx:
            first, last = prov[1, x, 0:1], prov[1, x, 15:16]
        else:
            first, last = edge_rows(low_edge if x < 0 else high_edge, j if x < 0 else x - nx)
        low1 = jnp.where(has_ylo, lowp[1:2], 0.0)
        high1 = jnp.where(has_yhi, highp[6:7], 0.0)
        value = jnp.concatenate([lowp, source[j], highp], axis=0)
        add = jnp.where(sub == 7, jnp.broadcast_to(first, (32, 128)), 0.0)
        add = jnp.where(sub == 8, jnp.broadcast_to(-low1, (32, 128)), add)
        add = jnp.where(sub == 23, jnp.broadcast_to(high1, (32, 128)), add)
        add = jnp.where(sub == 24, jnp.broadcast_to(-last, (32, 128)), add)
        value = masked((value + add) * (1.0 / 6.0), j)
        src.append(value)
        pa[j] = -value
    cur, new = pa, pb
    for sweep in range(1, 4):
        for j in range(sweep, rows - sweep):
            here = cur[j]
            up, down = zshift(here, lane)
            total = (cur[j - 1] + cur[j + 1]) + (pltpu.roll(here, 1, 0) + pltpu.roll(here, 31, 0))
            total = total + (up + down)
            new[j] = masked(total * (1.0 / 6.0) - src[j], j)
        cur, new = new, cur
    return cur, halo


def step_kernel(prov, x1, x2, source, y1, y2, spread, prov2, source2, out1, out2, pa, pb, ux, xlo, xhi, fromlow, fromhigh, tolow, tohigh):
    pick(x1, x2, xlo, xhi, "gx")
    pick(y1, y2, fromlow, fromhigh, "gy")
    nx = prov.shape[1]
    p, halo = solve(prov, xlo, xhi, source, fromlow, fromhigh, pa, pb)
    has_xlo, has_xhi, has_ylo, has_yhi = edge_flags()
    sub = lax.broadcasted_iota(jnp.int32, (32, 128), 0)
    lane = lax.broadcasted_iota(jnp.int32, (32, 128), 1)
    inside = ((sub >= 8) | has_ylo) & ((sub < 24) | has_yhi)
    for x in range(-1, nx + 1):
        j = x + halo
        here = p[j]
        up, down = zshift(here, lane)
        slopes = (
            p[j + 1] - p[j - 1],
            pltpu.roll(here, 31, 0) - pltpu.roll(here, 1, 0),
            up - down,
        )
        keep = inside
        if x < 0:
            keep = inside & has_xlo
        elif x >= nx:
            keep = inside & has_xhi
        lowp, highp = fromlow[j], fromhigh[j]
        for c in range(3):
            mid = xlo[halo + c] if x < 0 else xhi[halo + c] if x >= nx else prov[c, x]
            wide = jnp.concatenate(
                [pltpu.roll(lowp, 7 - c, 0), mid, pltpu.roll(highp, 3 - c, 0)], axis=0
            )
            ux[c, x + 1] = jnp.where(keep, wide - 0.25 * slopes[c], 0.0)
    lane16 = lax.broadcasted_iota(jnp.int32, (16, 128), 1)
    for c in range(3):
        for x in range(nx):
            here = ux[c, x + 1]
            ys = pltpu.roll(here, 1, 0) + pltpu.roll(here, 31, 0)
            mid = here[8:24]
            up, down = zshift(mid, lane16)
            total = (ux[c, x, 8:24] + ux[c, x + 2, 8:24]) + ys[8:24] + (up + down)
            pull = spread[c, x] - spread[3, x] * mid
            value = mid + 0.5 * (0.2 * (total - 6.0 * mid) + pull)
            prov2[c, x] = value
    divergence(lambda c, x: prov2[c, x], nx, source2, tolow, tohigh, (0,))
    place(tolow, tohigh, out1, out2, "gx")


def step_call(prov, xlo, xhi, source, fromlow, fromhigh, spread):
    _, nx, ny, nz = prov.shape
    rows = source.shape[0]
    return pl.pallas_call(
        step_kernel,
        out_shape=(
            jax.ShapeDtypeStruct(prov.shape, F32),
            jax.ShapeDtypeStruct((nx, ny, nz), F32),
            jax.ShapeDtypeStruct((HALO2 + 2, ny, nz), F32),
            jax.ShapeDtypeStruct((HALO2 + 2, ny, nz), F32),
        ),
        in_specs=[pl.BlockSpec(memory_space=VMEM)] * 7,
        out_specs=(pl.BlockSpec(memory_space=VMEM),) * 4,
        scratch_shapes=[
            VMEM((rows, 32, nz), F32),
            VMEM((rows, 32, nz), F32),
            VMEM((3, nx + 2, 32, nz), F32),
        ]
        + [VMEM(xlo.shape, F32)] * 2
        + [VMEM(fromlow.shape, F32)] * 2
        + [VMEM((HALO2 + 2, ny, nz), F32)] * 2,
        compiler_params=pltpu.CompilerParams(vmem_limit_bytes=12 << 20),
        name="step",
    )(prov, xlo, xhi, source, fromlow, fromhigh, spread)


DENSE, SPARSE = 11, 5


def last_kernel(prov, x1, x2, source, y1, y2, arrived, vel, picked, pa, pb, table, xlo, xhi, fromlow, fromhigh):
    pick(x1, x2, xlo, xhi, "gx")
    pick(y1, y2, fromlow, fromhigh, "gy")
    nx = prov.shape[1]
    senders = arrived.shape[0]
    p, halo = solve(prov, xlo, xhi, source, fromlow, fromhigh, pa, pb)
    lane16 = lax.broadcasted_iota(jnp.int32, (16, 128), 1)
    for x in range(nx):
        j = x + halo
        here = p[j]
        mid = here[8:24]
        up, down = zshift(mid, lane16)
        slopes = (
            p[j + 1, 8:24] - p[j - 1, 8:24],
            (pltpu.roll(here, 31, 0) - pltpu.roll(here, 1, 0))[8:24],
            up - down,
        )
        for c in range(3):
            value = prov[c, x] - 0.25 * slopes[c]
            vel[c, x] = value
            hi, lo = split(value)
            r = 64 * c + 16 * (x % 4)
            k = 128 * (x // 4)
            table[r : r + 16, k : k + 128] = hi
            table[192 + r : 192 + r + 16, k : k + 128] = lo
    rows8 = lax.broadcasted_iota(jnp.int32, (8, 128), 0)
    iota_r = lax.broadcasted_iota(jnp.int32, (256, 128), 0).astype(F32).astype(BF16)
    iota_c = lax.broadcasted_iota(jnp.int32, (64, 128), 0)
    one, zero = jnp.ones((), BF16), jnp.zeros((), BF16)

    def slot(e, c):
        k = 128 * (3 * e + c)
        return slice(k, k + 128)

    def dense(first):
        hot, cols = [], []
        for s in range(DENSE):
            number = arrived[first + s].astype(jnp.int32)
            rowf = ((number >> 13) * 128 + (number & 127)).astype(F32)
            col = (number >> 7) & 63
            for e in range(2):
                q = 4 * e + 3
                rr = jnp.broadcast_to(rowf[q : q + 1], (256, 128)).astype(BF16)
                hot.append(jnp.where(iota_r == rr, one, zero))
                cols.append(col[q : q + 1])
        got = jnp.dot(table[...], jnp.concatenate(hot, axis=1), preferred_element_type=F32)
        for s in range(DENSE):
            for e in range(2):
                k = 128 * (2 * s + e)
                mask = iota_c == jnp.broadcast_to(cols[2 * s + e], (64, 128))
                for c in range(3):
                    val = got[64 * c : 64 * c + 64, k : k + 128] + got[192 + 64 * c : 256 + 64 * c, k : k + 128]
                    val = jnp.where(mask, val, 0.0)
                    picked[first + s, :, slot(e, c)] = jnp.sum(val, axis=0, keepdims=True)

    def sparse(first):
        for s in range(SPARSE):
            number = arrived[first + s].astype(jnp.int32)
            for e in range(2):
                q = 4 * e + 3
                cell = jnp.broadcast_to(number[q : q + 1], (8, 128))
                z = cell & 127
                column = (cell >> 7) - rows8
                acc = [jnp.zeros((8, 128), F32) for _ in range(3)]
                for g in range(2 * nx):
                    mask = column == 8 * g
                    for c in range(3):
                        field = vel[c, g // 2, 8 * (g % 2) : 8 * (g % 2) + 8, :]
                        got = jnp.take_along_axis(field, z, axis=1, mode="promise_in_bounds")
                        acc[c] = jnp.where(mask, got, acc[c])
                for c in range(3):
                    picked[first + s, :, slot(e, c)] = jnp.sum(acc[c], axis=0, keepdims=True)

    def loop(i, carry):
        first = i * (DENSE + SPARSE)
        sparse(first)
        dense(first + SPARSE)
        return carry

    lax.fori_loop(0, senders // (DENSE + SPARSE), loop, 0)


def last_call(prov, xlo, xhi, source, fromlow, fromhigh, arrived):
    _, nx, ny, nz = prov.shape
    rows = source.shape[0]
    return pl.pallas_call(
        last_kernel,
        out_shape=(
            jax.ShapeDtypeStruct(prov.shape, F32),
            jax.ShapeDtypeStruct((arrived.shape[0], 1, 6 * nz), F32),
        ),
        in_specs=[pl.BlockSpec(memory_space=VMEM)] * 7,
        out_specs=(pl.BlockSpec(memory_space=VMEM),) * 2,
        scratch_shapes=[
            VMEM((rows, 32, nz), F32),
            VMEM((rows, 32, nz), F32),
            VMEM((384, 256), BF16),
        ]
        + [VMEM(xlo.shape, F32)] * 2
        + [VMEM(fromlow.shape, F32)] * 2,
        compiler_params=pltpu.CompilerParams(vmem_limit_bytes=28 << 20),
        name="last",
    )(prov, xlo, xhi, source, fromlow, fromhigh, arrived)


def pairs(axis, second):
    nx, ny = lax.axis_size("gx"), lax.axis_size("gy")
    out = []
    for i in range(nx):
        for j in range(ny):
            k, count = (i, nx) if axis == "gx" else (j, ny)
            other = ((k + 1) ^ 1) - 1 if second else k ^ 1
            if 0 <= other < count:
                to = (other, j) if axis == "gx" else (i, other)
            else:
                to = (i, j ^ 1) if axis == "gx" else (i ^ 1, j)
            out.append((i * ny + j, to[0] * ny + to[1]))
    return out


def swap(first, second, axis):
    both = ("gx", "gy")
    return (
        lax.ppermute(first, both, pairs(axis, False)),
        lax.ppermute(second, both, pairs(axis, True)),
    )


def body(velocity, marker_force, marker_cell, block_brick):
    devices = lax.axis_size("gx") * lax.axis_size("gy")
    blocks = marker_cell.shape[0]
    axes = ("gx", "gy")
    even_x, even_y = is_even("gx"), is_even("gy")
    outgoing, target = pack(block_brick.reshape(blocks), marker_force, marker_cell, devices)
    low, high = velocity[:, 0], velocity[:, -1]
    first, second = jnp.where(even_x, high, low), jnp.where(even_x, low, high)
    target = jnp.minimum(target, 2 * devices - 1)
    first, second, target = lax.optimization_barrier((first, second, target))
    x1, x2 = swap(first, second, "gx")
    low, high = velocity[:, :, 0], velocity[:, :, -1]
    y1, y2 = swap(jnp.where(even_y, high, low), jnp.where(even_y, low, high), "gy")
    arrived = lax.all_to_all(outgoing, axes, split_axis=0, concat_axis=0, tiled=True)
    prov, spread, brick, out1, out2 = spread_call(arrived, velocity, x1, x2, y1, y2)
    x1, x2 = swap(out1, out2, "gx")
    source, out1, out2 = edges_call(prov, brick, x1, x2, ALL)
    y1, y2 = swap(out1, out2, "gy")
    prov, brick, out1, out2 = step_call(prov, x1, x2, source, y1, y2, spread)
    x1, x2 = swap(out1, out2, "gx")
    source, out1, out2 = edges_call(prov, brick, x1, x2, (0,))
    y1, y2 = swap(out1, out2, "gy")
    final, picked = last_call(prov, x1, x2, source, y1, y2, arrived)
    back = lax.all_to_all(picked, axes, split_axis=0, concat_axis=0, tiled=True)
    return final, unpack(target, back, blocks)


def solution(mesh):
    return jax.shard_map(
        body,
        mesh=mesh,
        in_specs=(
            P(None, "gx", "gy", None),
            P(None, ("gx", "gy"), None),
            P(("gx", "gy"), None),
            P(("gx", "gy"), None),
        ),
        out_specs=(P(None, "gx", "gy", None), P(None, ("gx", "gy"), None)),
        check_vma=False,
    )
```

```python
import functools

import jax
import jax.numpy as jnp
from jax import lax
from jax.experimental import pallas as pl
from jax.experimental.pallas import tpu as pltpu
from jax.sharding import PartitionSpec as P


F32 = jnp.float32
BF16 = jnp.bfloat16
F8 = jnp.float8_e4m3fn
VMEM = pltpu.VMEM
SMEM = pltpu.SMEM


def pack_kernel(bb_any, force_any, cell_any, out, tgt, bb, force, cell, cnt, comb, sems):
    devices = out.shape[0]
    blocks = force.shape[1]
    copies = [
        pltpu.make_async_copy(src, dst, sems.at[i])
        for i, (src, dst) in enumerate(((bb_any, bb), (force_any, force), (cell_any, cell)))
    ]
    for copy in copies:
        copy.start()
    sub = lax.broadcasted_iota(jnp.int32, out.shape, 1)
    out[...] = jnp.where(sub % 4 == 3, -1.0, 0.0)

    def clear(i, carry):
        cnt[i] = 0
        return carry

    lax.fori_loop(0, devices, clear, 0, unroll=8)
    copies[0].wait()

    def slots(k, carry):
        for i in range(8):
            d = bb[8 * k + i]
            e = cnt[d]
            cnt[d] = e + 1
            tgt[8 * k + i] = 2 * d + e
        return carry

    lax.fori_loop(0, blocks // 8, slots, 0)
    copies[1].wait()
    copies[2].wait()
    for k in range(0, blocks, 8):
        for c in range(3):
            comb[pl.ds(8 * k + c, 8, 8), :] = force[c, k : k + 8, :]
        comb[pl.ds(8 * k + 3, 8, 8), :] = cell[k : k + 8, :].astype(F32)

    def eight(k, carry):
        first = pl.multiple_of(8 * k, 8)
        where = [tgt[first + i] for i in range(8)]
        rows = [comb[pl.ds(pl.multiple_of(8 * (first + i), 8), 4), :] for i in range(8)]
        for t, value in zip(where, rows):
            out[t >> 1, pl.ds(4 * (t & 1), 4), :] = value
        return carry

    lax.fori_loop(0, blocks // 8, eight, 0)


def pack(block_brick, force, cell, devices):
    blocks, width = cell.shape
    return pl.pallas_call(
        pack_kernel,
        out_shape=(
            jax.ShapeDtypeStruct((devices, 8, width), F32),
            jax.ShapeDtypeStruct((blocks,), jnp.int32),
        ),
        in_specs=[pl.BlockSpec(memory_space=pl.ANY)] * 3,
        out_specs=(pl.BlockSpec(memory_space=VMEM), pl.BlockSpec(memory_space=SMEM)),
        scratch_shapes=[
            SMEM((blocks,), jnp.int32),
            VMEM(force.shape, F32),
            VMEM(cell.shape, jnp.int32),
            SMEM((devices,), jnp.int32),
            VMEM((8 * blocks, width), F32),
            pltpu.SemaphoreType.DMA((3,)),
        ],
        name="pack",
    )(block_brick, force, cell)


def unpack_kernel(tgt, back, out):
    blocks, width = out.shape[1:]

    def eight(k, carry):
        first = pl.multiple_of(8 * k, 8)
        rows = []
        for i in range(8):
            t = tgt[first + i]
            base = pl.multiple_of((t & 1) * 3 * width, 128)
            rows.append([back[t >> 1, :, pl.ds(base + c * width, width)] for c in range(3)])
        for c in range(3):
            for i in range(8):
                out[c, pl.ds(first + i, 1), :] = rows[i][c]
        return carry

    lax.fori_loop(0, blocks // 8, eight, 0)


def unpack(tgt, back, blocks):
    return pl.pallas_call(
        unpack_kernel,
        out_shape=jax.ShapeDtypeStruct((3, blocks, back.shape[2] // 6), F32),
        in_specs=[pl.BlockSpec(memory_space=SMEM), pl.BlockSpec(memory_space=VMEM)],
        out_specs=pl.BlockSpec(memory_space=VMEM),
        compiler_params=pltpu.CompilerParams(vmem_limit_bytes=6 << 20),
        name="unpack",
    )(tgt, back)


def zshift(v, lane):
    size = v.shape[-1]
    up = jnp.where(lane == size - 1, 0.0, pltpu.roll(v, size - 1, v.ndim - 1))
    down = jnp.where(lane == 0, 0.0, pltpu.roll(v, 1, v.ndim - 1))
    return up, down


def edge_flags():
    gx, gy = lax.axis_index("gx"), lax.axis_index("gy")
    nx, ny = lax.axis_size("gx"), lax.axis_size("gy")
    return gx > 0, gx < nx - 1, gy > 0, gy < ny - 1


def is_even(axis):
    return lax.axis_index(axis) % 2 == 0


def place(low, high, first, second, axis):
    even = is_even(axis)
    first[...] = jnp.where(even, high[...], low[...])
    second[...] = jnp.where(even, low[...], high[...])


def pick(first, second, low, high, axis):
    even = is_even(axis)
    low[...] = jnp.where(even, second[...], first[...])
    high[...] = jnp.where(even, first[...], second[...])


def divergence(p, nx, source, tolow, tohigh, comps):
    depth = tolow.shape[0] - len(comps) - 1
    lane = lax.broadcasted_iota(jnp.int32, (16, 128), 1)
    sub = lax.broadcasted_iota(jnp.int32, (16, 128), 0)
    low_edges = jnp.zeros((16, 128), F32)
    high_edges = jnp.zeros((16, 128), F32)
    for x in range(nx):
        p1 = p(1, x)
        ym = jnp.where(sub == 0, 0.0, pltpu.roll(p1, 1, 0))
        yp = jnp.where(sub == 15, 0.0, pltpu.roll(p1, 15, 0))
        up, down = zshift(p(2, x), lane)
        value = (yp - ym) + (up - down)
        if x < nx - 1:
            value = value + p(0, x + 1)
        if x > 0:
            value = value - p(0, x - 1)
        source[x] = value
        first, last = jnp.broadcast_to(p1[0:1], (16, 128)), jnp.broadcast_to(p1[15:16], (16, 128))
        if x < depth:
            tolow[x] = value
            low_edges = jnp.where(sub == 2 * x, first, jnp.where(sub == 2 * x + 1, last, low_edges))
        k = x - (nx - depth)
        if k >= 0:
            tohigh[k] = value
            high_edges = jnp.where(sub == 2 * k, first, jnp.where(sub == 2 * k + 1, last, high_edges))
    for i, c in enumerate(comps):
        tolow[depth + i] = p(c, 0)
        tohigh[depth + i] = p(c, nx - 1)
    tolow[depth + len(comps)] = low_edges
    tohigh[depth + len(comps)] = high_edges


ALL = (0, 1, 2)
HALO1, HALO2 = 5, 4
CHUNK = 16


def split(v):
    hi = v.astype(BF16)
    lo = (v - hi.astype(F32)).astype(BF16)
    return hi, lo


def one_hots(packet, scale, iota_r, iota_c):
    number = packet.astype(jnp.int32)
    row = ((number >> 13) * 128 + (number & 127)).astype(F32)
    col = ((number >> 7) & 63).astype(F32)
    rest = packet * scale
    parts = []
    for part in range(3):
        near = rest.astype(F8).astype(F32)
        parts.append(near)
        rest = (rest - near) * 16.0
    one, zero = jnp.ones((), BF16), jnp.zeros((), BF16)
    out = []
    for e in range(2):
        q = 4 * e + 3
        rr = jnp.broadcast_to(row[q : q + 1], (256, 128)).astype(BF16)
        hot = jnp.where(iota_r == rr, one, zero).astype(F8)
        cc = jnp.broadcast_to(col[q : q + 1], (64, 128)).astype(BF16)
        mask = iota_c == cc
        rows = []
        for c in range(3):
            p = 4 * e + c
            for src in parts:
                val = jnp.broadcast_to(src[p : p + 1], (64, 128)).astype(BF16)
                rows.append(jnp.where(mask, val, zero).astype(F8))
        rows.append(jnp.where(mask, one, zero).astype(F8))
        out.append((hot, jnp.concatenate(rows, axis=0)))
    return out


def spread_kernel(arrived, vel, x1, x2, y1, y2, prov, spread, source, out1, out2, acc, xlo, xhi, ylo, yhi, tolow, tohigh):
    pick(x1, x2, xlo, xhi, "gx")
    pick(y1, y2, ylo, yhi, "gy")
    senders = arrived.shape[0]
    iota_r = lax.broadcasted_iota(jnp.int32, (256, 128), 0).astype(F32).astype(BF16)
    iota_c = lax.broadcasted_iota(jnp.int32, (64, 128), 0).astype(F32).astype(BF16)
    dims = (((1,), (1,)), ((), ()))
    acc[...] = jnp.zeros_like(acc)
    sub = lax.broadcasted_iota(jnp.int32, arrived.shape, 1)
    size = jnp.max(jnp.where(sub % 4 == 3, 0.0, jnp.abs(arrived[...])))
    size = jnp.maximum(jnp.full((8, 128), size), 1e-30)
    scale = 4.0 / size

    def loop(i, carry):
        hots, vals = [], []
        for s in range(CHUNK):
            for hot, val in one_hots(arrived[i * CHUNK + s], scale, iota_r, iota_c):
                hots.append(hot)
                vals.append(val)
        acc[...] += lax.dot_general(
            jnp.concatenate(vals, axis=1), jnp.concatenate(hots, axis=1), dims, preferred_element_type=F32
        )
        return carry

    lax.fori_loop(0, senders // CHUNK, loop, 0)
    unit = size[0:1, 0:1] * 0.25
    for c in range(3):
        k = 192 * c
        total = acc[k : k + 64] + (acc[k + 64 : k + 128] + acc[k + 128 : k + 192] * 0.0625) * 0.0625
        total = total * unit
        spread[c, 0:4] = total[:, :128].reshape(4, 16, 128)
        spread[c, 4:8] = total[:, 128:].reshape(4, 16, 128)
    spread[3, 0:4] = acc[576:640, :128].reshape(4, 16, 128)
    spread[3, 4:8] = acc[576:640, 128:].reshape(4, 16, 128)
    has_xlo, has_xhi, has_ylo, has_yhi = edge_flags()
    lane = lax.broadcasted_iota(jnp.int32, (16, 128), 1)
    sub = lax.broadcasted_iota(jnp.int32, (16, 128), 0)
    nx = vel.shape[1]
    for c in range(3):
        for x in range(nx):
            here = vel[c, x]
            before = vel[c, x - 1] if x else jnp.where(has_xlo, xlo[c], 0.0)
            after = vel[c, x + 1] if x < nx - 1 else jnp.where(has_xhi, xhi[c], 0.0)
            left = jnp.broadcast_to(jnp.where(has_ylo, ylo[c, x : x + 1], 0.0), (16, 128))
            right = jnp.broadcast_to(jnp.where(has_yhi, yhi[c, x : x + 1], 0.0), (16, 128))
            ym = jnp.where(sub == 0, left, pltpu.roll(here, 1, 0))
            yp = jnp.where(sub == 15, right, pltpu.roll(here, 15, 0))
            up, down = zshift(here, lane)
            total = ((after + before) + (yp + ym)) + (up + down)
            value = here + 0.5 * (0.2 * (total - 6.0 * here) + spread[c, x])
            prov[c, x] = value
    divergence(lambda c, x: prov[c, x], nx, source, tolow, tohigh, ALL)
    place(tolow, tohigh, out1, out2, "gx")


def spread_call(arrived, vel, xlo, xhi, ylo, yhi):
    _, nx, ny, nz = vel.shape
    return pl.pallas_call(
        spread_kernel,
        out_shape=(
            jax.ShapeDtypeStruct(vel.shape, F32),
            jax.ShapeDtypeStruct((4, nx, ny, nz), F32),
            jax.ShapeDtypeStruct((nx, ny, nz), F32),
            jax.ShapeDtypeStruct((HALO1 + 4, ny, nz), F32),
            jax.ShapeDtypeStruct((HALO1 + 4, ny, nz), F32),
        ),
        in_specs=[pl.BlockSpec(memory_space=VMEM)] * 6,
        out_specs=(pl.BlockSpec(memory_space=VMEM),) * 5,
        scratch_shapes=[VMEM((640, 256), F32)]
        + [VMEM((3, ny, nz), F32)] * 2
        + [VMEM((3, nx, nz), F32)] * 2
        + [VMEM((HALO1 + 4, ny, nz), F32)] * 2,
        compiler_params=pltpu.CompilerParams(vmem_limit_bytes=28 << 20),
        name="spread",
    )(arrived, vel, xlo, xhi, ylo, yhi)


def edges_kernel(comps, prov, brick, x1, x2, source, out1, out2, xlo, xhi, tolow, tohigh):
    pick(x1, x2, xlo, xhi, "gx")
    nx = brick.shape[0]
    rows = source.shape[0]
    halo = (rows - nx) // 2
    has_xlo, has_xhi, _, _ = edge_flags()
    sub8 = lax.broadcasted_iota(jnp.int32, (8, 128), 0)
    zero8 = jnp.zeros((8, 128), F32)
    low_edge, high_edge = xlo[halo + len(comps)], xhi[halo + len(comps)]
    for j in range(rows):
        x = j - halo
        if x < 0:
            value = xlo[j]
            if x == -1:
                value = value + prov[0, 0]
        elif x < nx:
            value = brick[x]
            if x == 0:
                value = value - jnp.where(has_xlo, xlo[halo], 0.0)
            if x == nx - 1:
                value = value + jnp.where(has_xhi, xhi[halo], 0.0)
        else:
            value = xhi[x - nx]
            if x == nx:
                value = value - prov[0, nx - 1]
        source[j] = value
        high, low = value[8:16], value[0:8]
        if 0 <= x < nx:
            for c in comps if 1 in comps else (1,):
                p = prov[c, x]
                high = jnp.where(sub8 == c, pltpu.roll(p[8:16], c + 1, 0), high)
                low = jnp.where(sub8 == 5 + c, pltpu.roll(p[0:8], 5 + c, 0), low)
        else:
            first, last = edge_rows(low_edge if x < 0 else high_edge, j if x < 0 else x - nx)
            high = jnp.where(sub8 == 1, jnp.broadcast_to(last, (8, 128)), high)
            low = jnp.where(sub8 == 6, jnp.broadcast_to(first, (8, 128)), low)
            if 1 in comps and x in (-1, nx):
                packet = xlo if x < 0 else xhi
                for c in (0, 2):
                    p = packet[halo + c]
                    high = jnp.where(sub8 == c, pltpu.roll(p[8:16], c + 1, 0), high)
                    low = jnp.where(sub8 == 5 + c, pltpu.roll(p[0:8], 5 + c, 0), low)
        tohigh[j] = high
        tolow[j] = low
    place(tolow, tohigh, out1, out2, "gy")


def edge_rows(edges, k):
    return edges[2 * k : 2 * k + 1], edges[2 * k + 1 : 2 * k + 2]


def edges_call(prov, brick, xlo, xhi, comps):
    nx, ny, nz = brick.shape
    rows = nx + 2 * (xlo.shape[0] - len(comps) - 1)
    return pl.pallas_call(
        functools.partial(edges_kernel, comps),
        out_shape=(
            jax.ShapeDtypeStruct((rows, ny, nz), F32),
            jax.ShapeDtypeStruct((rows, 8, nz), F32),
            jax.ShapeDtypeStruct((rows, 8, nz), F32),
        ),
        in_specs=[pl.BlockSpec(memory_space=VMEM)] * 4,
        out_specs=(pl.BlockSpec(memory_space=VMEM),) * 3,
        scratch_shapes=[VMEM(xlo.shape, F32)] * 2 + [VMEM((rows, 8, nz), F32)] * 2,
        compiler_params=pltpu.CompilerParams(vmem_limit_bytes=6 << 20),
        name="edges",
    )(prov, brick, xlo, xhi)


def solve(prov, xlo, xhi, source, fromlow, fromhigh, pa, pb):
    rows = source.shape[0]
    nx = prov.shape[1]
    halo = (rows - nx) // 2
    low_edge, high_edge = xlo[xlo.shape[0] - 1], xhi[xhi.shape[0] - 1]
    has_xlo, has_xhi, has_ylo, has_yhi = edge_flags()
    sub = lax.broadcasted_iota(jnp.int32, (32, 128), 0)
    lane = lax.broadcasted_iota(jnp.int32, (32, 128), 1)
    inside = ((sub >= 8) | has_ylo) & ((sub < 24) | has_yhi)

    def masked(v, j):
        keep = inside
        if j < halo:
            keep = inside & has_xlo
        elif j >= halo + nx:
            keep = inside & has_xhi
        return jnp.where(keep, v, 0.0)

    src = []
    for j in range(rows):
        lowp = fromlow[j]
        highp = fromhigh[j]
        x = j - halo
        if 0 <= x < nx:
            first, last = prov[1, x, 0:1], prov[1, x, 15:16]
        else:
            first, last = edge_rows(low_edge if x < 0 else high_edge, j if x < 0 else x - nx)
        low1 = jnp.where(has_ylo, lowp[1:2], 0.0)
        high1 = jnp.where(has_yhi, highp[6:7], 0.0)
        value = jnp.concatenate([lowp, source[j], highp], axis=0)
        add = jnp.where(sub == 7, jnp.broadcast_to(first, (32, 128)), 0.0)
        add = jnp.where(sub == 8, jnp.broadcast_to(-low1, (32, 128)), add)
        add = jnp.where(sub == 23, jnp.broadcast_to(high1, (32, 128)), add)
        add = jnp.where(sub == 24, jnp.broadcast_to(-last, (32, 128)), add)
        value = masked((value + add) * (1.0 / 6.0), j)
        src.append(value)
        pa[j] = -value
    cur, new = pa, pb
    for sweep in range(1, 4):
        for j in range(sweep, rows - sweep):
            here = cur[j]
            up, down = zshift(here, lane)
            total = (cur[j - 1] + cur[j + 1]) + (pltpu.roll(here, 1, 0) + pltpu.roll(here, 31, 0))
            total = total + (up + down)
            new[j] = masked(total * (1.0 / 6.0) - src[j], j)
        cur, new = new, cur
    return cur, halo


def step_kernel(prov, x1, x2, source, y1, y2, spread, prov2, source2, out1, out2, pa, pb, ux, xlo, xhi, fromlow, fromhigh, tolow, tohigh):
    pick(x1, x2, xlo, xhi, "gx")
    pick(y1, y2, fromlow, fromhigh, "gy")
    nx = prov.shape[1]
    p, halo = solve(prov, xlo, xhi, source, fromlow, fromhigh, pa, pb)
    has_xlo, has_xhi, has_ylo, has_yhi = edge_flags()
    sub = lax.broadcasted_iota(jnp.int32, (32, 128), 0)
    lane = lax.broadcasted_iota(jnp.int32, (32, 128), 1)
    inside = ((sub >= 8) | has_ylo) & ((sub < 24) | has_yhi)
    for x in range(-1, nx + 1):
        j = x + halo
        here = p[j]
        up, down = zshift(here, lane)
        slopes = (
            p[j + 1] - p[j - 1],
            pltpu.roll(here, 31, 0) - pltpu.roll(here, 1, 0),
            up - down,
        )
        keep = inside
        if x < 0:
            keep = inside & has_xlo
        elif x >= nx:
            keep = inside & has_xhi
        lowp, highp = fromlow[j], fromhigh[j]
        for c in range(3):
            mid = xlo[halo + c] if x < 0 else xhi[halo + c] if x >= nx else prov[c, x]
            wide = jnp.concatenate(
                [pltpu.roll(lowp, 7 - c, 0), mid, pltpu.roll(highp, 3 - c, 0)], axis=0
            )
            ux[c, x + 1] = jnp.where(keep, wide - 0.25 * slopes[c], 0.0)
    lane16 = lax.broadcasted_iota(jnp.int32, (16, 128), 1)
    for c in range(3):
        for x in range(nx):
            here = ux[c, x + 1]
            ys = pltpu.roll(here, 1, 0) + pltpu.roll(here, 31, 0)
            mid = here[8:24]
            up, down = zshift(mid, lane16)
            total = (ux[c, x, 8:24] + ux[c, x + 2, 8:24]) + ys[8:24] + (up + down)
            pull = spread[c, x] - spread[3, x] * mid
            value = mid + 0.5 * (0.2 * (total - 6.0 * mid) + pull)
            prov2[c, x] = value
    divergence(lambda c, x: prov2[c, x], nx, source2, tolow, tohigh, (0,))
    place(tolow, tohigh, out1, out2, "gx")


def step_call(prov, xlo, xhi, source, fromlow, fromhigh, spread):
    _, nx, ny, nz = prov.shape
    rows = source.shape[0]
    return pl.pallas_call(
        step_kernel,
        out_shape=(
            jax.ShapeDtypeStruct(prov.shape, F32),
            jax.ShapeDtypeStruct((nx, ny, nz), F32),
            jax.ShapeDtypeStruct((HALO2 + 2, ny, nz), F32),
            jax.ShapeDtypeStruct((HALO2 + 2, ny, nz), F32),
        ),
        in_specs=[pl.BlockSpec(memory_space=VMEM)] * 7,
        out_specs=(pl.BlockSpec(memory_space=VMEM),) * 4,
        scratch_shapes=[
            VMEM((rows, 32, nz), F32),
            VMEM((rows, 32, nz), F32),
            VMEM((3, nx + 2, 32, nz), F32),
        ]
        + [VMEM(xlo.shape, F32)] * 2
        + [VMEM(fromlow.shape, F32)] * 2
        + [VMEM((HALO2 + 2, ny, nz), F32)] * 2,
        compiler_params=pltpu.CompilerParams(vmem_limit_bytes=12 << 20),
        name="step",
    )(prov, xlo, xhi, source, fromlow, fromhigh, spread)


DENSE, SPARSE = 11, 5


def last_kernel(prov, x1, x2, source, y1, y2, arrived, vel, picked, pa, pb, table, xlo, xhi, fromlow, fromhigh):
    pick(x1, x2, xlo, xhi, "gx")
    pick(y1, y2, fromlow, fromhigh, "gy")
    nx = prov.shape[1]
    senders = arrived.shape[0]
    p, halo = solve(prov, xlo, xhi, source, fromlow, fromhigh, pa, pb)
    lane16 = lax.broadcasted_iota(jnp.int32, (16, 128), 1)
    for x in range(nx):
        j = x + halo
        here = p[j]
        mid = here[8:24]
        up, down = zshift(mid, lane16)
        slopes = (
            p[j + 1, 8:24] - p[j - 1, 8:24],
            (pltpu.roll(here, 31, 0) - pltpu.roll(here, 1, 0))[8:24],
            up - down,
        )
        for c in range(3):
            value = prov[c, x] - 0.25 * slopes[c]
            vel[c, x] = value
            hi, lo = split(value)
            r = 64 * c + 16 * (x % 4)
            k = 128 * (x // 4)
            table[r : r + 16, k : k + 128] = hi
            table[192 + r : 192 + r + 16, k : k + 128] = lo
    rows8 = lax.broadcasted_iota(jnp.int32, (8, 128), 0)
    iota_r = lax.broadcasted_iota(jnp.int32, (256, 128), 0).astype(F32).astype(BF16)
    iota_c = lax.broadcasted_iota(jnp.int32, (64, 128), 0)
    one, zero = jnp.ones((), BF16), jnp.zeros((), BF16)

    def slot(e, c):
        k = 128 * (3 * e + c)
        return slice(k, k + 128)

    def dense(first):
        hot, cols = [], []
        for s in range(DENSE):
            number = arrived[first + s].astype(jnp.int32)
            rowf = ((number >> 13) * 128 + (number & 127)).astype(F32)
            col = (number >> 7) & 63
            for e in range(2):
                q = 4 * e + 3
                rr = jnp.broadcast_to(rowf[q : q + 1], (256, 128)).astype(BF16)
                hot.append(jnp.where(iota_r == rr, one, zero))
                cols.append(col[q : q + 1])
        got = jnp.dot(table[...], jnp.concatenate(hot, axis=1), preferred_element_type=F32)
        for s in range(DENSE):
            for e in range(2):
                k = 128 * (2 * s + e)
                mask = iota_c == jnp.broadcast_to(cols[2 * s + e], (64, 128))
                for c in range(3):
                    val = got[64 * c : 64 * c + 64, k : k + 128] + got[192 + 64 * c : 256 + 64 * c, k : k + 128]
                    val = jnp.where(mask, val, 0.0)
                    picked[first + s, :, slot(e, c)] = jnp.sum(val, axis=0, keepdims=True)

    def sparse(first):
        for s in range(SPARSE):
            number = arrived[first + s].astype(jnp.int32)
            for e in range(2):
                q = 4 * e + 3
                cell = jnp.broadcast_to(number[q : q + 1], (8, 128))
                z = cell & 127
                column = (cell >> 7) - rows8
                acc = [jnp.zeros((8, 128), F32) for _ in range(3)]
                for g in range(2 * nx):
                    mask = column == 8 * g
                    for c in range(3):
                        field = vel[c, g // 2, 8 * (g % 2) : 8 * (g % 2) + 8, :]
                        got = jnp.take_along_axis(field, z, axis=1, mode="promise_in_bounds")
                        acc[c] = jnp.where(mask, got, acc[c])
                for c in range(3):
                    picked[first + s, :, slot(e, c)] = jnp.sum(acc[c], axis=0, keepdims=True)

    def loop(i, carry):
        first = i * (DENSE + SPARSE)
        sparse(first)
        dense(first + SPARSE)
        return carry

    lax.fori_loop(0, senders // (DENSE + SPARSE), loop, 0)


def last_call(prov, xlo, xhi, source, fromlow, fromhigh, arrived):
    _, nx, ny, nz = prov.shape
    rows = source.shape[0]
    return pl.pallas_call(
        last_kernel,
        out_shape=(
            jax.ShapeDtypeStruct(prov.shape, F32),
            jax.ShapeDtypeStruct((arrived.shape[0], 1, 6 * nz), F32),
        ),
        in_specs=[pl.BlockSpec(memory_space=VMEM)] * 7,
        out_specs=(pl.BlockSpec(memory_space=VMEM),) * 2,
        scratch_shapes=[
            VMEM((rows, 32, nz), F32),
            VMEM((rows, 32, nz), F32),
            VMEM((384, 256), BF16),
        ]
        + [VMEM(xlo.shape, F32)] * 2
        + [VMEM(fromlow.shape, F32)] * 2,
        compiler_params=pltpu.CompilerParams(vmem_limit_bytes=28 << 20),
        name="last",
    )(prov, xlo, xhi, source, fromlow, fromhigh, arrived)


def pairs(axis, second):
    nx, ny = lax.axis_size("gx"), lax.axis_size("gy")
    out = []
    for i in range(nx):
        for j in range(ny):
            k, count = (i, nx) if axis == "gx" else (j, ny)
            other = ((k + 1) ^ 1) - 1 if second else k ^ 1
            if 0 <= other < count:
                to = (other, j) if axis == "gx" else (i, other)
            else:
                to = (i, j ^ 1) if axis == "gx" else (i ^ 1, j)
            out.append((i * ny + j, to[0] * ny + to[1]))
    return out


def swap(first, second, axis):
    both = ("gx", "gy")
    return (
        lax.ppermute(first, both, pairs(axis, False)),
        lax.ppermute(second, both, pairs(axis, True)),
    )


def body(velocity, marker_force, marker_cell, block_brick):
    devices = lax.axis_size("gx") * lax.axis_size("gy")
    blocks = marker_cell.shape[0]
    axes = ("gx", "gy")
    even_x, even_y = is_even("gx"), is_even("gy")
    outgoing, target = pack(block_brick.reshape(blocks), marker_force, marker_cell, devices)
    low, high = velocity[:, 0], velocity[:, -1]
    first, second = jnp.where(even_x, high, low), jnp.where(even_x, low, high)
    target = jnp.minimum(target, 2 * devices - 1)
    first, second, target = lax.optimization_barrier((first, second, target))
    x1, x2 = swap(first, second, "gx")
    low, high = velocity[:, :, 0], velocity[:, :, -1]
    y1, y2 = swap(jnp.where(even_y, high, low), jnp.where(even_y, low, high), "gy")
    arrived = lax.all_to_all(outgoing, axes, split_axis=0, concat_axis=0, tiled=True)
    prov, spread, brick, out1, out2 = spread_call(arrived, velocity, x1, x2, y1, y2)
    x1, x2 = swap(out1, out2, "gx")
    source, out1, out2 = edges_call(prov, brick, x1, x2, ALL)
    y1, y2 = swap(out1, out2, "gy")
    prov, brick, out1, out2 = step_call(prov, x1, x2, source, y1, y2, spread)
    x1, x2 = swap(out1, out2, "gx")
    source, out1, out2 = edges_call(prov, brick, x1, x2, (0,))
    y1, y2 = swap(out1, out2, "gy")
    final, picked = last_call(prov, x1, x2, source, y1, y2, arrived)
    back = lax.all_to_all(picked, axes, split_axis=0, concat_axis=0, tiled=True)
    return final, unpack(target, back, blocks)


def solution(mesh):
    return jax.shard_map(
        body,
        mesh=mesh,
        in_specs=(
            P(None, "gx", "gy", None),
            P(None, ("gx", "gy"), None),
            P(("gx", "gy"), None),
            P(("gx", "gy"), None),
        ),
        out_specs=(P(None, "gx", "gy", None), P(None, ("gx", "gy"), None)),
        check_vma=False,
    )
```

```python
import functools

import jax
import jax.numpy as jnp
from jax import lax
from jax.experimental import pallas as pl
from jax.experimental.pallas import tpu as pltpu
from jax.sharding import PartitionSpec as P


F32 = jnp.float32
BF16 = jnp.bfloat16
F8 = jnp.float8_e4m3fn
VMEM = pltpu.VMEM
SMEM = pltpu.SMEM


def pack_kernel(bb_any, force_any, cell_any, out, tgt, bb, force, cell, cnt, comb, sems):
    devices = out.shape[0]
    blocks = force.shape[1]
    copies = [
        pltpu.make_async_copy(src, dst, sems.at[i])
        for i, (src, dst) in enumerate(((bb_any, bb), (force_any, force), (cell_any, cell)))
    ]
    for copy in copies:
        copy.start()
    sub = lax.broadcasted_iota(jnp.int32, out.shape, 1)
    out[...] = jnp.where(sub % 4 == 3, -1.0, 0.0)

    def clear(i, carry):
        cnt[i] = 0
        return carry

    lax.fori_loop(0, devices, clear, 0, unroll=8)
    copies[0].wait()

    def slots(k, carry):
        for i in range(8):
            d = bb[8 * k + i]
            e = cnt[d]
            cnt[d] = e + 1
            tgt[8 * k + i] = 2 * d + e
        return carry

    lax.fori_loop(0, blocks // 8, slots, 0)
    copies[1].wait()
    copies[2].wait()
    for k in range(0, blocks, 8):
        for c in range(3):
            comb[pl.ds(8 * k + c, 8, 8), :] = force[c, k : k + 8, :]
        comb[pl.ds(8 * k + 3, 8, 8), :] = cell[k : k + 8, :].astype(F32)

    def eight(k, carry):
        first = pl.multiple_of(8 * k, 8)
        where = [tgt[first + i] for i in range(8)]
        rows = [comb[pl.ds(pl.multiple_of(8 * (first + i), 8), 4), :] for i in range(8)]
        for t, value in zip(where, rows):
            out[t >> 1, pl.ds(4 * (t & 1), 4), :] = value
        return carry

    lax.fori_loop(0, blocks // 8, eight, 0)


def pack(block_brick, force, cell, devices):
    blocks, width = cell.shape
    return pl.pallas_call(
        pack_kernel,
        out_shape=(
            jax.ShapeDtypeStruct((devices, 8, width), F32),
            jax.ShapeDtypeStruct((blocks,), jnp.int32),
        ),
        in_specs=[pl.BlockSpec(memory_space=pl.ANY)] * 3,
        out_specs=(pl.BlockSpec(memory_space=VMEM), pl.BlockSpec(memory_space=SMEM)),
        scratch_shapes=[
            SMEM((blocks,), jnp.int32),
            VMEM(force.shape, F32),
            VMEM(cell.shape, jnp.int32),
            SMEM((devices,), jnp.int32),
            VMEM((8 * blocks, width), F32),
            pltpu.SemaphoreType.DMA((3,)),
        ],
        name="pack",
    )(block_brick, force, cell)


def unpack_kernel(tgt, back, out):
    blocks, width = out.shape[1:]

    def eight(k, carry):
        first = pl.multiple_of(8 * k, 8)
        rows = []
        for i in range(8):
            t = tgt[first + i]
            rows.append([back[t, :, c * width : (c + 1) * width] for c in range(3)])
        for c in range(3):
            for i in range(8):
                out[c, pl.ds(first + i, 1), :] = rows[i][c]
        return carry

    lax.fori_loop(0, blocks // 8, eight, 0)


def unpack(tgt, back, blocks):
    return pl.pallas_call(
        unpack_kernel,
        out_shape=jax.ShapeDtypeStruct((3, blocks, back.shape[2] // 3), F32),
        in_specs=[pl.BlockSpec(memory_space=SMEM), pl.BlockSpec(memory_space=VMEM)],
        out_specs=pl.BlockSpec(memory_space=VMEM),
        compiler_params=pltpu.CompilerParams(vmem_limit_bytes=6 << 20),
        name="unpack",
    )(tgt, back)


def zshift(v, lane):
    size = v.shape[-1]
    up = jnp.where(lane == size - 1, 0.0, pltpu.roll(v, size - 1, v.ndim - 1))
    down = jnp.where(lane == 0, 0.0, pltpu.roll(v, 1, v.ndim - 1))
    return up, down


def edge_flags():
    gx, gy = lax.axis_index("gx"), lax.axis_index("gy")
    nx, ny = lax.axis_size("gx"), lax.axis_size("gy")
    return gx > 0, gx < nx - 1, gy > 0, gy < ny - 1


def is_even(axis):
    return lax.axis_index(axis) % 2 == 0


def place(low, high, first, second, axis):
    even = is_even(axis)
    first[...] = jnp.where(even, high[...], low[...])
    second[...] = jnp.where(even, low[...], high[...])


def pick(first, second, low, high, axis):
    even = is_even(axis)
    low[...] = jnp.where(even, second[...], first[...])
    high[...] = jnp.where(even, first[...], second[...])


def divergence(p, nx, source, tolow, tohigh, comps):
    depth = tolow.shape[0] - len(comps) - 1
    lane = lax.broadcasted_iota(jnp.int32, (16, 128), 1)
    sub = lax.broadcasted_iota(jnp.int32, (16, 128), 0)
    low_edges = jnp.zeros((16, 128), F32)
    high_edges = jnp.zeros((16, 128), F32)
    for x in range(nx):
        p1 = p(1, x)
        ym = jnp.where(sub == 0, 0.0, pltpu.roll(p1, 1, 0))
        yp = jnp.where(sub == 15, 0.0, pltpu.roll(p1, 15, 0))
        up, down = zshift(p(2, x), lane)
        value = (yp - ym) + (up - down)
        if x < nx - 1:
            value = value + p(0, x + 1)
        if x > 0:
            value = value - p(0, x - 1)
        source[x] = value
        first, last = jnp.broadcast_to(p1[0:1], (16, 128)), jnp.broadcast_to(p1[15:16], (16, 128))
        if x < depth:
            tolow[x] = value
            low_edges = jnp.where(sub == 2 * x, first, jnp.where(sub == 2 * x + 1, last, low_edges))
        k = x - (nx - depth)
        if k >= 0:
            tohigh[k] = value
            high_edges = jnp.where(sub == 2 * k, first, jnp.where(sub == 2 * k + 1, last, high_edges))
    for i, c in enumerate(comps):
        tolow[depth + i] = p(c, 0)
        tohigh[depth + i] = p(c, nx - 1)
    tolow[depth + len(comps)] = low_edges
    tohigh[depth + len(comps)] = high_edges


ALL = (0, 1, 2)
HALO1, HALO2 = 5, 4
CHUNK = 32


def split(v):
    hi = v.astype(BF16)
    lo = (v - hi.astype(F32)).astype(BF16)
    return hi, lo


def one_hots(packet, scale, iota_r, iota_c):
    number = packet.astype(jnp.int32)
    row = ((number >> 13) * 128 + (number & 127)).astype(F32)
    col = ((number >> 7) & 63).astype(F32)
    rest = packet * scale
    parts = []
    for part in range(3):
        near = rest.astype(F8).astype(F32)
        parts.append(near)
        rest = (rest - near) * 16.0
    one, zero = jnp.ones((), BF16), jnp.zeros((), BF16)
    out = []
    for e in range(2):
        q = 4 * e + 3
        rr = jnp.broadcast_to(row[q : q + 1], (256, 128)).astype(BF16)
        hot = jnp.where(iota_r == rr, one, zero).astype(F8)
        cc = jnp.broadcast_to(col[q : q + 1], (64, 128)).astype(BF16)
        mask = iota_c == cc
        rows = []
        for c in range(3):
            p = 4 * e + c
            for src in parts:
                val = jnp.broadcast_to(src[p : p + 1], (64, 128)).astype(BF16)
                rows.append(jnp.where(mask, val, zero).astype(F8))
        rows.append(jnp.where(mask, one, zero).astype(F8))
        out.append((hot, jnp.concatenate(rows, axis=0)))
    return out


def spread_kernel(arrived, vel, x1, x2, y1, y2, prov, spread, source, out1, out2, acc, xlo, xhi, ylo, yhi, tolow, tohigh):
    pick(x1, x2, xlo, xhi, "gx")
    pick(y1, y2, ylo, yhi, "gy")
    senders = arrived.shape[0]
    iota_r = lax.broadcasted_iota(jnp.int32, (256, 128), 0).astype(F32).astype(BF16)
    iota_c = lax.broadcasted_iota(jnp.int32, (64, 128), 0).astype(F32).astype(BF16)
    dims = (((1,), (1,)), ((), ()))
    acc[...] = jnp.zeros_like(acc)
    sub = lax.broadcasted_iota(jnp.int32, arrived.shape, 1)
    size = jnp.max(jnp.where(sub % 4 == 3, 0.0, jnp.abs(arrived[...])))
    size = jnp.maximum(jnp.full((8, 128), size), 1e-30)
    scale = 4.0 / size

    def loop(i, carry):
        hots, vals = [], []
        for s in range(CHUNK):
            for hot, val in one_hots(arrived[i * CHUNK + s], scale, iota_r, iota_c):
                hots.append(hot)
                vals.append(val)
        acc[...] += lax.dot_general(
            jnp.concatenate(vals, axis=1), jnp.concatenate(hots, axis=1), dims, preferred_element_type=F32
        )
        return carry

    lax.fori_loop(0, senders // CHUNK, loop, 0)
    unit = size[0:1, 0:1] * 0.25
    for c in range(3):
        k = 192 * c
        total = acc[k : k + 64] + (acc[k + 64 : k + 128] + acc[k + 128 : k + 192] * 0.0625) * 0.0625
        total = total * unit
        spread[c, 0:4] = total[:, :128].reshape(4, 16, 128)
        spread[c, 4:8] = total[:, 128:].reshape(4, 16, 128)
    spread[3, 0:4] = acc[576:640, :128].reshape(4, 16, 128)
    spread[3, 4:8] = acc[576:640, 128:].reshape(4, 16, 128)
    has_xlo, has_xhi, has_ylo, has_yhi = edge_flags()
    lane = lax.broadcasted_iota(jnp.int32, (16, 128), 1)
    sub = lax.broadcasted_iota(jnp.int32, (16, 128), 0)
    nx = vel.shape[1]
    for c in range(3):
        for x in range(nx):
            here = vel[c, x]
            before = vel[c, x - 1] if x else jnp.where(has_xlo, xlo[c], 0.0)
            after = vel[c, x + 1] if x < nx - 1 else jnp.where(has_xhi, xhi[c], 0.0)
            left = jnp.broadcast_to(jnp.where(has_ylo, ylo[c, x : x + 1], 0.0), (16, 128))
            right = jnp.broadcast_to(jnp.where(has_yhi, yhi[c, x : x + 1], 0.0), (16, 128))
            ym = jnp.where(sub == 0, left, pltpu.roll(here, 1, 0))
            yp = jnp.where(sub == 15, right, pltpu.roll(here, 15, 0))
            up, down = zshift(here, lane)
            total = ((after + before) + (yp + ym)) + (up + down)
            value = here + 0.5 * (0.2 * (total - 6.0 * here) + spread[c, x])
            prov[c, x] = value
    divergence(lambda c, x: prov[c, x], nx, source, tolow, tohigh, ALL)
    place(tolow, tohigh, out1, out2, "gx")


def spread_call(arrived, vel, xlo, xhi, ylo, yhi):
    _, nx, ny, nz = vel.shape
    return pl.pallas_call(
        spread_kernel,
        out_shape=(
            jax.ShapeDtypeStruct(vel.shape, F32),
            jax.ShapeDtypeStruct((4, nx, ny, nz), F32),
            jax.ShapeDtypeStruct((nx, ny, nz), F32),
            jax.ShapeDtypeStruct((HALO1 + 4, ny, nz), F32),
            jax.ShapeDtypeStruct((HALO1 + 4, ny, nz), F32),
        ),
        in_specs=[pl.BlockSpec(memory_space=VMEM)] * 6,
        out_specs=(pl.BlockSpec(memory_space=VMEM),) * 5,
        scratch_shapes=[VMEM((640, 256), F32)]
        + [VMEM((3, ny, nz), F32)] * 2
        + [VMEM((3, nx, nz), F32)] * 2
        + [VMEM((HALO1 + 4, ny, nz), F32)] * 2,
        compiler_params=pltpu.CompilerParams(vmem_limit_bytes=28 << 20),
        name="spread",
    )(arrived, vel, xlo, xhi, ylo, yhi)


def edges_kernel(comps, prov, brick, x1, x2, source, out1, out2, xlo, xhi, tolow, tohigh):
    pick(x1, x2, xlo, xhi, "gx")
    nx = brick.shape[0]
    rows = source.shape[0]
    halo = (rows - nx) // 2
    has_xlo, has_xhi, _, _ = edge_flags()
    sub8 = lax.broadcasted_iota(jnp.int32, (8, 128), 0)
    zero8 = jnp.zeros((8, 128), F32)
    low_edge, high_edge = xlo[halo + len(comps)], xhi[halo + len(comps)]
    for j in range(rows):
        x = j - halo
        if x < 0:
            value = xlo[j]
            if x == -1:
                value = value + prov[0, 0]
        elif x < nx:
            value = brick[x]
            if x == 0:
                value = value - jnp.where(has_xlo, xlo[halo], 0.0)
            if x == nx - 1:
                value = value + jnp.where(has_xhi, xhi[halo], 0.0)
        else:
            value = xhi[x - nx]
            if x == nx:
                value = value - prov[0, nx - 1]
        source[j] = value
        high, low = value[8:16], value[0:8]
        if 0 <= x < nx:
            for c in comps if 1 in comps else (1,):
                p = prov[c, x]
                high = jnp.where(sub8 == c, pltpu.roll(p[8:16], c + 1, 0), high)
                low = jnp.where(sub8 == 5 + c, pltpu.roll(p[0:8], 5 + c, 0), low)
        else:
            first, last = edge_rows(low_edge if x < 0 else high_edge, j if x < 0 else x - nx)
            high = jnp.where(sub8 == 1, jnp.broadcast_to(last, (8, 128)), high)
            low = jnp.where(sub8 == 6, jnp.broadcast_to(first, (8, 128)), low)
            if 1 in comps and x in (-1, nx):
                packet = xlo if x < 0 else xhi
                for c in (0, 2):
                    p = packet[halo + c]
                    high = jnp.where(sub8 == c, pltpu.roll(p[8:16], c + 1, 0), high)
                    low = jnp.where(sub8 == 5 + c, pltpu.roll(p[0:8], 5 + c, 0), low)
        tohigh[j] = high
        tolow[j] = low
    place(tolow, tohigh, out1, out2, "gy")


def edge_rows(edges, k):
    return edges[2 * k : 2 * k + 1], edges[2 * k + 1 : 2 * k + 2]


def edges_call(prov, brick, xlo, xhi, comps):
    nx, ny, nz = brick.shape
    rows = nx + 2 * (xlo.shape[0] - len(comps) - 1)
    return pl.pallas_call(
        functools.partial(edges_kernel, comps),
        out_shape=(
            jax.ShapeDtypeStruct((rows, ny, nz), F32),
            jax.ShapeDtypeStruct((rows, 8, nz), F32),
            jax.ShapeDtypeStruct((rows, 8, nz), F32),
        ),
        in_specs=[pl.BlockSpec(memory_space=VMEM)] * 4,
        out_specs=(pl.BlockSpec(memory_space=VMEM),) * 3,
        scratch_shapes=[VMEM(xlo.shape, F32)] * 2 + [VMEM((rows, 8, nz), F32)] * 2,
        compiler_params=pltpu.CompilerParams(vmem_limit_bytes=6 << 20),
        name="edges",
    )(prov, brick, xlo, xhi)


def solve(prov, xlo, xhi, source, fromlow, fromhigh, pa, pb):
    rows = source.shape[0]
    nx = prov.shape[1]
    halo = (rows - nx) // 2
    low_edge, high_edge = xlo[xlo.shape[0] - 1], xhi[xhi.shape[0] - 1]
    has_xlo, has_xhi, has_ylo, has_yhi = edge_flags()
    sub = lax.broadcasted_iota(jnp.int32, (32, 128), 0)
    lane = lax.broadcasted_iota(jnp.int32, (32, 128), 1)
    inside = ((sub >= 8) | has_ylo) & ((sub < 24) | has_yhi)

    def masked(v, j):
        keep = inside
        if j < halo:
            keep = inside & has_xlo
        elif j >= halo + nx:
            keep = inside & has_xhi
        return jnp.where(keep, v, 0.0)

    src = []
    for j in range(rows):
        lowp = fromlow[j]
        highp = fromhigh[j]
        x = j - halo
        if 0 <= x < nx:
            first, last = prov[1, x, 0:1], prov[1, x, 15:16]
        else:
            first, last = edge_rows(low_edge if x < 0 else high_edge, j if x < 0 else x - nx)
        low1 = jnp.where(has_ylo, lowp[1:2], 0.0)
        high1 = jnp.where(has_yhi, highp[6:7], 0.0)
        value = jnp.concatenate([lowp, source[j], highp], axis=0)
        add = jnp.where(sub == 7, jnp.broadcast_to(first, (32, 128)), 0.0)
        add = jnp.where(sub == 8, jnp.broadcast_to(-low1, (32, 128)), add)
        add = jnp.where(sub == 23, jnp.broadcast_to(high1, (32, 128)), add)
        add = jnp.where(sub == 24, jnp.broadcast_to(-last, (32, 128)), add)
        value = masked((value + add) * (1.0 / 6.0), j)
        src.append(value)
        pa[j] = -value
    cur, new = pa, pb
    for sweep in range(1, 4):
        for j in range(sweep, rows - sweep):
            here = cur[j]
            up, down = zshift(here, lane)
            total = (cur[j - 1] + cur[j + 1]) + (pltpu.roll(here, 1, 0) + pltpu.roll(here, 31, 0))
            total = total + (up + down)
            new[j] = masked(total * (1.0 / 6.0) - src[j], j)
        cur, new = new, cur
    return cur, halo


def step_kernel(prov, x1, x2, source, y1, y2, spread, prov2, source2, out1, out2, pa, pb, ux, xlo, xhi, fromlow, fromhigh, tolow, tohigh):
    pick(x1, x2, xlo, xhi, "gx")
    pick(y1, y2, fromlow, fromhigh, "gy")
    nx = prov.shape[1]
    p, halo = solve(prov, xlo, xhi, source, fromlow, fromhigh, pa, pb)
    has_xlo, has_xhi, has_ylo, has_yhi = edge_flags()
    sub = lax.broadcasted_iota(jnp.int32, (32, 128), 0)
    lane = lax.broadcasted_iota(jnp.int32, (32, 128), 1)
    inside = ((sub >= 8) | has_ylo) & ((sub < 24) | has_yhi)
    for x in range(-1, nx + 1):
        j = x + halo
        here = p[j]
        up, down = zshift(here, lane)
        slopes = (
            p[j + 1] - p[j - 1],
            pltpu.roll(here, 31, 0) - pltpu.roll(here, 1, 0),
            up - down,
        )
        keep = inside
        if x < 0:
            keep = inside & has_xlo
        elif x >= nx:
            keep = inside & has_xhi
        lowp, highp = fromlow[j], fromhigh[j]
        for c in range(3):
            mid = xlo[halo + c] if x < 0 else xhi[halo + c] if x >= nx else prov[c, x]
            wide = jnp.concatenate(
                [pltpu.roll(lowp, 7 - c, 0), mid, pltpu.roll(highp, 3 - c, 0)], axis=0
            )
            ux[c, x + 1] = jnp.where(keep, wide - 0.25 * slopes[c], 0.0)
    lane16 = lax.broadcasted_iota(jnp.int32, (16, 128), 1)
    for c in range(3):
        for x in range(nx):
            here = ux[c, x + 1]
            ys = pltpu.roll(here, 1, 0) + pltpu.roll(here, 31, 0)
            mid = here[8:24]
            up, down = zshift(mid, lane16)
            total = (ux[c, x, 8:24] + ux[c, x + 2, 8:24]) + ys[8:24] + (up + down)
            pull = spread[c, x] - spread[3, x] * mid
            value = mid + 0.5 * (0.2 * (total - 6.0 * mid) + pull)
            prov2[c, x] = value
    divergence(lambda c, x: prov2[c, x], nx, source2, tolow, tohigh, (0,))
    place(tolow, tohigh, out1, out2, "gx")


def step_call(prov, xlo, xhi, source, fromlow, fromhigh, spread):
    _, nx, ny, nz = prov.shape
    rows = source.shape[0]
    return pl.pallas_call(
        step_kernel,
        out_shape=(
            jax.ShapeDtypeStruct(prov.shape, F32),
            jax.ShapeDtypeStruct((nx, ny, nz), F32),
            jax.ShapeDtypeStruct((HALO2 + 2, ny, nz), F32),
            jax.ShapeDtypeStruct((HALO2 + 2, ny, nz), F32),
        ),
        in_specs=[pl.BlockSpec(memory_space=VMEM)] * 7,
        out_specs=(pl.BlockSpec(memory_space=VMEM),) * 4,
        scratch_shapes=[
            VMEM((rows, 32, nz), F32),
            VMEM((rows, 32, nz), F32),
            VMEM((3, nx + 2, 32, nz), F32),
        ]
        + [VMEM(xlo.shape, F32)] * 2
        + [VMEM(fromlow.shape, F32)] * 2
        + [VMEM((HALO2 + 2, ny, nz), F32)] * 2,
        compiler_params=pltpu.CompilerParams(vmem_limit_bytes=12 << 20),
        name="step",
    )(prov, xlo, xhi, source, fromlow, fromhigh, spread)


DENSE, SPARSE = 11, 5


def last_kernel(prov, x1, x2, source, y1, y2, arrived, vel, picked, pa, pb, table, xlo, xhi, fromlow, fromhigh):
    pick(x1, x2, xlo, xhi, "gx")
    pick(y1, y2, fromlow, fromhigh, "gy")
    nx = prov.shape[1]
    senders = arrived.shape[0]
    p, halo = solve(prov, xlo, xhi, source, fromlow, fromhigh, pa, pb)
    lane16 = lax.broadcasted_iota(jnp.int32, (16, 128), 1)
    for x in range(nx):
        j = x + halo
        here = p[j]
        mid = here[8:24]
        up, down = zshift(mid, lane16)
        slopes = (
            p[j + 1, 8:24] - p[j - 1, 8:24],
            (pltpu.roll(here, 31, 0) - pltpu.roll(here, 1, 0))[8:24],
            up - down,
        )
        for c in range(3):
            value = prov[c, x] - 0.25 * slopes[c]
            vel[c, x] = value
            hi, lo = split(value)
            r = 64 * c + 16 * (x % 4)
            k = 128 * (x // 4)
            table[r : r + 16, k : k + 128] = hi
            table[192 + r : 192 + r + 16, k : k + 128] = lo
    rows8 = lax.broadcasted_iota(jnp.int32, (8, 128), 0)
    iota_r = lax.broadcasted_iota(jnp.int32, (256, 128), 0).astype(F32).astype(BF16)
    iota_c = lax.broadcasted_iota(jnp.int32, (64, 128), 0)
    one, zero = jnp.ones((), BF16), jnp.zeros((), BF16)

    def dense(first):
        hot, cols = [], []
        for s in range(DENSE):
            number = arrived[first + s].astype(jnp.int32)
            rowf = ((number >> 13) * 128 + (number & 127)).astype(F32)
            col = (number >> 7) & 63
            for e in range(2):
                q = 4 * e + 3
                rr = jnp.broadcast_to(rowf[q : q + 1], (256, 128)).astype(BF16)
                hot.append(jnp.where(iota_r == rr, one, zero))
                cols.append(col[q : q + 1])
        got = jnp.dot(table[...], jnp.concatenate(hot, axis=1), preferred_element_type=F32)
        for s in range(DENSE):
            for e in range(2):
                k = 128 * (2 * s + e)
                mask = iota_c == jnp.broadcast_to(cols[2 * s + e], (64, 128))
                for c in range(3):
                    val = got[64 * c : 64 * c + 64, k : k + 128] + got[192 + 64 * c : 256 + 64 * c, k : k + 128]
                    val = jnp.where(mask, val, 0.0)
                    picked[2 * (first + s) + e, :, 128 * c : 128 * c + 128] = jnp.sum(val, axis=0, keepdims=True)

    def sparse(first):
        for s in range(SPARSE):
            number = arrived[first + s].astype(jnp.int32)
            for e in range(2):
                q = 4 * e + 3
                cell = jnp.broadcast_to(number[q : q + 1], (8, 128))
                z = cell & 127
                column = (cell >> 7) - rows8
                acc = [jnp.zeros((8, 128), F32) for _ in range(3)]
                for g in range(2 * nx):
                    mask = column == 8 * g
                    for c in range(3):
                        field = vel[c, g // 2, 8 * (g % 2) : 8 * (g % 2) + 8, :]
                        got = jnp.take_along_axis(field, z, axis=1, mode="promise_in_bounds")
                        acc[c] = jnp.where(mask, got, acc[c])
                for c in range(3):
                    picked[2 * (first + s) + e, :, 128 * c : 128 * c + 128] = jnp.sum(acc[c], axis=0, keepdims=True)

    def loop(i, carry):
        first = i * (DENSE + SPARSE)
        sparse(first)
        dense(first + SPARSE)
        return carry

    lax.fori_loop(0, senders // (DENSE + SPARSE), loop, 0)


def last_call(prov, xlo, xhi, source, fromlow, fromhigh, arrived):
    _, nx, ny, nz = prov.shape
    rows = source.shape[0]
    return pl.pallas_call(
        last_kernel,
        out_shape=(
            jax.ShapeDtypeStruct(prov.shape, F32),
            jax.ShapeDtypeStruct((2 * arrived.shape[0], 1, 3 * nz), F32),
        ),
        in_specs=[pl.BlockSpec(memory_space=VMEM)] * 7,
        out_specs=(pl.BlockSpec(memory_space=VMEM),) * 2,
        scratch_shapes=[
            VMEM((rows, 32, nz), F32),
            VMEM((rows, 32, nz), F32),
            VMEM((384, 256), BF16),
        ]
        + [VMEM(xlo.shape, F32)] * 2
        + [VMEM(fromlow.shape, F32)] * 2,
        compiler_params=pltpu.CompilerParams(vmem_limit_bytes=28 << 20),
        name="last",
    )(prov, xlo, xhi, source, fromlow, fromhigh, arrived)


def pairs(axis, second):
    nx, ny = lax.axis_size("gx"), lax.axis_size("gy")
    out = []
    for i in range(nx):
        for j in range(ny):
            k, count = (i, nx) if axis == "gx" else (j, ny)
            other = ((k + 1) ^ 1) - 1 if second else k ^ 1
            if 0 <= other < count:
                to = (other, j) if axis == "gx" else (i, other)
            else:
                to = (i, j ^ 1) if axis == "gx" else (i ^ 1, j)
            out.append((i * ny + j, to[0] * ny + to[1]))
    return out


def swap(first, second, axis):
    both = ("gx", "gy")
    return (
        lax.ppermute(first, both, pairs(axis, False)),
        lax.ppermute(second, both, pairs(axis, True)),
    )


def body(velocity, marker_force, marker_cell, block_brick):
    devices = lax.axis_size("gx") * lax.axis_size("gy")
    blocks = marker_cell.shape[0]
    axes = ("gx", "gy")
    even_x, even_y = is_even("gx"), is_even("gy")
    outgoing, target = pack(block_brick.reshape(blocks), marker_force, marker_cell, devices)
    low, high = velocity[:, 0], velocity[:, -1]
    first, second = jnp.where(even_x, high, low), jnp.where(even_x, low, high)
    target = jnp.minimum(target, 2 * devices - 1)
    first, second, target = lax.optimization_barrier((first, second, target))
    x1, x2 = swap(first, second, "gx")
    low, high = velocity[:, :, 0], velocity[:, :, -1]
    y1, y2 = swap(jnp.where(even_y, high, low), jnp.where(even_y, low, high), "gy")
    arrived = lax.all_to_all(outgoing, axes, split_axis=0, concat_axis=0, tiled=True)
    prov, spread, brick, out1, out2 = spread_call(arrived, velocity, x1, x2, y1, y2)
    x1, x2 = swap(out1, out2, "gx")
    source, out1, out2 = edges_call(prov, brick, x1, x2, ALL)
    y1, y2 = swap(out1, out2, "gy")
    prov, brick, out1, out2 = step_call(prov, x1, x2, source, y1, y2, spread)
    x1, x2 = swap(out1, out2, "gx")
    source, out1, out2 = edges_call(prov, brick, x1, x2, (0,))
    y1, y2 = swap(out1, out2, "gy")
    final, picked = last_call(prov, x1, x2, source, y1, y2, arrived)
    back = lax.all_to_all(picked, axes, split_axis=0, concat_axis=0, tiled=True)
    return final, unpack(target, back, blocks)


def solution(mesh):
    return jax.shard_map(
        body,
        mesh=mesh,
        in_specs=(
            P(None, "gx", "gy", None),
            P(None, ("gx", "gy"), None),
            P(("gx", "gy"), None),
            P(("gx", "gy"), None),
        ),
        out_specs=(P(None, "gx", "gy", None), P(None, ("gx", "gy"), None)),
        check_vma=False,
    )
```

```python
import functools

import jax
import jax.numpy as jnp
from jax import lax
from jax.experimental import pallas as pl
from jax.experimental.pallas import tpu as pltpu
from jax.sharding import PartitionSpec as P


F32 = jnp.float32
BF16 = jnp.bfloat16
F8 = jnp.float8_e4m3fn
VMEM = pltpu.VMEM
SMEM = pltpu.SMEM


def pack_kernel(bb_any, force_any, cell_any, out, tgt, bb, force, cell, cnt, comb, sems):
    devices = out.shape[0]
    blocks = force.shape[1]
    copies = [
        pltpu.make_async_copy(src, dst, sems.at[i])
        for i, (src, dst) in enumerate(((bb_any, bb), (force_any, force), (cell_any, cell)))
    ]
    for copy in copies:
        copy.start()
    sub = lax.broadcasted_iota(jnp.int32, out.shape, 1)
    out[...] = jnp.where(sub % 4 == 3, -1.0, 0.0)

    def clear(i, carry):
        cnt[i] = 0
        return carry

    lax.fori_loop(0, devices, clear, 0, unroll=8)
    copies[0].wait()

    def slots(k, carry):
        for i in range(8):
            d = bb[8 * k + i]
            e = cnt[d]
            cnt[d] = e + 1
            tgt[8 * k + i] = 2 * d + e
        return carry

    lax.fori_loop(0, blocks // 8, slots, 0)
    copies[1].wait()
    copies[2].wait()
    for k in range(0, blocks, 8):
        for c in range(3):
            comb[pl.ds(8 * k + c, 8, 8), :] = force[c, k : k + 8, :]
        comb[pl.ds(8 * k + 3, 8, 8), :] = cell[k : k + 8, :].astype(F32)

    def eight(k, carry):
        first = pl.multiple_of(8 * k, 8)
        where = [tgt[first + i] for i in range(8)]
        rows = [comb[pl.ds(pl.multiple_of(8 * (first + i), 8), 4), :] for i in range(8)]
        for t, value in zip(where, rows):
            out[t >> 1, pl.ds(4 * (t & 1), 4), :] = value
        return carry

    lax.fori_loop(0, blocks // 8, eight, 0)


def pack(block_brick, force, cell, devices):
    blocks, width = cell.shape
    return pl.pallas_call(
        pack_kernel,
        out_shape=(
            jax.ShapeDtypeStruct((devices, 8, width), F32),
            jax.ShapeDtypeStruct((blocks,), jnp.int32),
        ),
        in_specs=[pl.BlockSpec(memory_space=pl.ANY)] * 3,
        out_specs=(pl.BlockSpec(memory_space=VMEM), pl.BlockSpec(memory_space=SMEM)),
        scratch_shapes=[
            SMEM((blocks,), jnp.int32),
            VMEM(force.shape, F32),
            VMEM(cell.shape, jnp.int32),
            SMEM((devices,), jnp.int32),
            VMEM((8 * blocks, width), F32),
            pltpu.SemaphoreType.DMA((3,)),
        ],
        name="pack",
    )(block_brick, force, cell)


def unpack_kernel(tgt, back, out):
    blocks, width = out.shape[1:]

    def eight(k, carry):
        first = pl.multiple_of(8 * k, 8)
        rows = []
        for i in range(8):
            t = tgt[first + i]
            rows.append([back[t, :, c * width : (c + 1) * width] for c in range(3)])
        for c in range(3):
            for i in range(8):
                out[c, pl.ds(first + i, 1), :] = rows[i][c]
        return carry

    lax.fori_loop(0, blocks // 8, eight, 0)


def unpack(tgt, back, blocks):
    return pl.pallas_call(
        unpack_kernel,
        out_shape=jax.ShapeDtypeStruct((3, blocks, back.shape[2] // 3), F32),
        in_specs=[pl.BlockSpec(memory_space=SMEM), pl.BlockSpec(memory_space=VMEM)],
        out_specs=pl.BlockSpec(memory_space=VMEM),
        compiler_params=pltpu.CompilerParams(vmem_limit_bytes=6 << 20),
        name="unpack",
    )(tgt, back)


def zshift(v, lane):
    size = v.shape[-1]
    up = jnp.where(lane == size - 1, 0.0, pltpu.roll(v, size - 1, v.ndim - 1))
    down = jnp.where(lane == 0, 0.0, pltpu.roll(v, 1, v.ndim - 1))
    return up, down


def edge_flags():
    gx, gy = lax.axis_index("gx"), lax.axis_index("gy")
    nx, ny = lax.axis_size("gx"), lax.axis_size("gy")
    return gx > 0, gx < nx - 1, gy > 0, gy < ny - 1


def is_even(axis):
    return lax.axis_index(axis) % 2 == 0


def place(low, high, first, second, axis):
    even = is_even(axis)
    first[...] = jnp.where(even, high[...], low[...])
    second[...] = jnp.where(even, low[...], high[...])


def pick(first, second, low, high, axis):
    even = is_even(axis)
    low[...] = jnp.where(even, second[...], first[...])
    high[...] = jnp.where(even, first[...], second[...])


def divergence(p, nx, source, tolow, tohigh, comps):
    depth = tolow.shape[0] - len(comps) - 1
    lane = lax.broadcasted_iota(jnp.int32, (16, 128), 1)
    sub = lax.broadcasted_iota(jnp.int32, (16, 128), 0)
    low_edges = jnp.zeros((16, 128), F32)
    high_edges = jnp.zeros((16, 128), F32)
    for x in range(nx):
        p1 = p(1, x)
        ym = jnp.where(sub == 0, 0.0, pltpu.roll(p1, 1, 0))
        yp = jnp.where(sub == 15, 0.0, pltpu.roll(p1, 15, 0))
        up, down = zshift(p(2, x), lane)
        value = (yp - ym) + (up - down)
        if x < nx - 1:
            value = value + p(0, x + 1)
        if x > 0:
            value = value - p(0, x - 1)
        source[x] = value
        first, last = jnp.broadcast_to(p1[0:1], (16, 128)), jnp.broadcast_to(p1[15:16], (16, 128))
        if x < depth:
            tolow[x] = value
            low_edges = jnp.where(sub == 2 * x, first, jnp.where(sub == 2 * x + 1, last, low_edges))
        k = x - (nx - depth)
        if k >= 0:
            tohigh[k] = value
            high_edges = jnp.where(sub == 2 * k, first, jnp.where(sub == 2 * k + 1, last, high_edges))
    for i, c in enumerate(comps):
        tolow[depth + i] = p(c, 0)
        tohigh[depth + i] = p(c, nx - 1)
    tolow[depth + len(comps)] = low_edges
    tohigh[depth + len(comps)] = high_edges


ALL = (0, 1, 2)
HALO1, HALO2 = 5, 4
CHUNK = 64


def split(v):
    hi = v.astype(BF16)
    lo = (v - hi.astype(F32)).astype(BF16)
    return hi, lo


def one_hots(packet, scale, iota_r, iota_c):
    number = packet.astype(jnp.int32)
    row = ((number >> 13) * 128 + (number & 127)).astype(F32)
    col = ((number >> 7) & 63).astype(F32)
    rest = packet * scale
    parts = []
    for part in range(3):
        near = rest.astype(F8).astype(F32)
        parts.append(near)
        rest = (rest - near) * 16.0
    one, zero = jnp.ones((), BF16), jnp.zeros((), BF16)
    out = []
    for e in range(2):
        q = 4 * e + 3
        rr = jnp.broadcast_to(row[q : q + 1], (256, 128)).astype(BF16)
        hot = jnp.where(iota_r == rr, one, zero).astype(F8)
        cc = jnp.broadcast_to(col[q : q + 1], (64, 128)).astype(BF16)
        mask = iota_c == cc
        rows = []
        for c in range(3):
            p = 4 * e + c
            for src in parts:
                val = jnp.broadcast_to(src[p : p + 1], (64, 128)).astype(BF16)
                rows.append(jnp.where(mask, val, zero).astype(F8))
        rows.append(jnp.where(mask, one, zero).astype(F8))
        out.append((hot, jnp.concatenate(rows, axis=0)))
    return out


def spread_kernel(arrived, vel, x1, x2, y1, y2, prov, spread, source, out1, out2, acc, xlo, xhi, ylo, yhi, tolow, tohigh):
    pick(x1, x2, xlo, xhi, "gx")
    pick(y1, y2, ylo, yhi, "gy")
    senders = arrived.shape[0]
    iota_r = lax.broadcasted_iota(jnp.int32, (256, 128), 0).astype(F32).astype(BF16)
    iota_c = lax.broadcasted_iota(jnp.int32, (64, 128), 0).astype(F32).astype(BF16)
    dims = (((1,), (1,)), ((), ()))
    acc[...] = jnp.zeros_like(acc)
    sub = lax.broadcasted_iota(jnp.int32, arrived.shape, 1)
    size = jnp.max(jnp.where(sub % 4 == 3, 0.0, jnp.abs(arrived[...])))
    size = jnp.maximum(jnp.full((8, 128), size), 1e-30)
    scale = 4.0 / size

    def loop(i, carry):
        hots, vals = [], []
        for s in range(CHUNK):
            for hot, val in one_hots(arrived[i * CHUNK + s], scale, iota_r, iota_c):
                hots.append(hot)
                vals.append(val)
        acc[...] += lax.dot_general(
            jnp.concatenate(vals, axis=1), jnp.concatenate(hots, axis=1), dims, preferred_element_type=F32
        )
        return carry

    lax.fori_loop(0, senders // CHUNK, loop, 0)
    unit = size[0:1, 0:1] * 0.25
    for c in range(3):
        k = 192 * c
        total = acc[k : k + 64] + (acc[k + 64 : k + 128] + acc[k + 128 : k + 192] * 0.0625) * 0.0625
        total = total * unit
        spread[c, 0:4] = total[:, :128].reshape(4, 16, 128)
        spread[c, 4:8] = total[:, 128:].reshape(4, 16, 128)
    spread[3, 0:4] = acc[576:640, :128].reshape(4, 16, 128)
    spread[3, 4:8] = acc[576:640, 128:].reshape(4, 16, 128)
    has_xlo, has_xhi, has_ylo, has_yhi = edge_flags()
    lane = lax.broadcasted_iota(jnp.int32, (16, 128), 1)
    sub = lax.broadcasted_iota(jnp.int32, (16, 128), 0)
    nx = vel.shape[1]
    for c in range(3):
        for x in range(nx):
            here = vel[c, x]
            before = vel[c, x - 1] if x else jnp.where(has_xlo, xlo[c], 0.0)
            after = vel[c, x + 1] if x < nx - 1 else jnp.where(has_xhi, xhi[c], 0.0)
            left = jnp.broadcast_to(jnp.where(has_ylo, ylo[c, x : x + 1], 0.0), (16, 128))
            right = jnp.broadcast_to(jnp.where(has_yhi, yhi[c, x : x + 1], 0.0), (16, 128))
            ym = jnp.where(sub == 0, left, pltpu.roll(here, 1, 0))
            yp = jnp.where(sub == 15, right, pltpu.roll(here, 15, 0))
            up, down = zshift(here, lane)
            total = ((after + before) + (yp + ym)) + (up + down)
            value = here + 0.5 * (0.2 * (total - 6.0 * here) + spread[c, x])
            prov[c, x] = value
    divergence(lambda c, x: prov[c, x], nx, source, tolow, tohigh, ALL)
    place(tolow, tohigh, out1, out2, "gx")


def spread_call(arrived, vel, xlo, xhi, ylo, yhi):
    _, nx, ny, nz = vel.shape
    return pl.pallas_call(
        spread_kernel,
        out_shape=(
            jax.ShapeDtypeStruct(vel.shape, F32),
            jax.ShapeDtypeStruct((4, nx, ny, nz), F32),
            jax.ShapeDtypeStruct((nx, ny, nz), F32),
            jax.ShapeDtypeStruct((HALO1 + 4, ny, nz), F32),
            jax.ShapeDtypeStruct((HALO1 + 4, ny, nz), F32),
        ),
        in_specs=[pl.BlockSpec(memory_space=VMEM)] * 6,
        out_specs=(pl.BlockSpec(memory_space=VMEM),) * 5,
        scratch_shapes=[VMEM((640, 256), F32)]
        + [VMEM((3, ny, nz), F32)] * 2
        + [VMEM((3, nx, nz), F32)] * 2
        + [VMEM((HALO1 + 4, ny, nz), F32)] * 2,
        compiler_params=pltpu.CompilerParams(vmem_limit_bytes=28 << 20),
        name="spread",
    )(arrived, vel, xlo, xhi, ylo, yhi)


def edges_kernel(comps, prov, brick, x1, x2, source, out1, out2, xlo, xhi, tolow, tohigh):
    pick(x1, x2, xlo, xhi, "gx")
    nx = brick.shape[0]
    rows = source.shape[0]
    halo = (rows - nx) // 2
    has_xlo, has_xhi, _, _ = edge_flags()
    sub8 = lax.broadcasted_iota(jnp.int32, (8, 128), 0)
    zero8 = jnp.zeros((8, 128), F32)
    low_edge, high_edge = xlo[halo + len(comps)], xhi[halo + len(comps)]
    for j in range(rows):
        x = j - halo
        if x < 0:
            value = xlo[j]
            if x == -1:
                value = value + prov[0, 0]
        elif x < nx:
            value = brick[x]
            if x == 0:
                value = value - jnp.where(has_xlo, xlo[halo], 0.0)
            if x == nx - 1:
                value = value + jnp.where(has_xhi, xhi[halo], 0.0)
        else:
            value = xhi[x - nx]
            if x == nx:
                value = value - prov[0, nx - 1]
        source[j] = value
        high, low = value[8:16], value[0:8]
        if 0 <= x < nx:
            for c in comps if 1 in comps else (1,):
                p = prov[c, x]
                high = jnp.where(sub8 == c, pltpu.roll(p[8:16], c + 1, 0), high)
                low = jnp.where(sub8 == 5 + c, pltpu.roll(p[0:8], 5 + c, 0), low)
        else:
            first, last = edge_rows(low_edge if x < 0 else high_edge, j if x < 0 else x - nx)
            high = jnp.where(sub8 == 1, jnp.broadcast_to(last, (8, 128)), high)
            low = jnp.where(sub8 == 6, jnp.broadcast_to(first, (8, 128)), low)
            if 1 in comps and x in (-1, nx):
                packet = xlo if x < 0 else xhi
                for c in (0, 2):
                    p = packet[halo + c]
                    high = jnp.where(sub8 == c, pltpu.roll(p[8:16], c + 1, 0), high)
                    low = jnp.where(sub8 == 5 + c, pltpu.roll(p[0:8], 5 + c, 0), low)
        tohigh[j] = high
        tolow[j] = low
    place(tolow, tohigh, out1, out2, "gy")


def edge_rows(edges, k):
    return edges[2 * k : 2 * k + 1], edges[2 * k + 1 : 2 * k + 2]


def edges_call(prov, brick, xlo, xhi, comps):
    nx, ny, nz = brick.shape
    rows = nx + 2 * (xlo.shape[0] - len(comps) - 1)
    return pl.pallas_call(
        functools.partial(edges_kernel, comps),
        out_shape=(
            jax.ShapeDtypeStruct((rows, ny, nz), F32),
            jax.ShapeDtypeStruct((rows, 8, nz), F32),
            jax.ShapeDtypeStruct((rows, 8, nz), F32),
        ),
        in_specs=[pl.BlockSpec(memory_space=VMEM)] * 4,
        out_specs=(pl.BlockSpec(memory_space=VMEM),) * 3,
        scratch_shapes=[VMEM(xlo.shape, F32)] * 2 + [VMEM((rows, 8, nz), F32)] * 2,
        compiler_params=pltpu.CompilerParams(vmem_limit_bytes=6 << 20),
        name="edges",
    )(prov, brick, xlo, xhi)


def solve(prov, xlo, xhi, source, fromlow, fromhigh, pa, pb):
    rows = source.shape[0]
    nx = prov.shape[1]
    halo = (rows - nx) // 2
    low_edge, high_edge = xlo[xlo.shape[0] - 1], xhi[xhi.shape[0] - 1]
    has_xlo, has_xhi, has_ylo, has_yhi = edge_flags()
    sub = lax.broadcasted_iota(jnp.int32, (32, 128), 0)
    lane = lax.broadcasted_iota(jnp.int32, (32, 128), 1)
    inside = ((sub >= 8) | has_ylo) & ((sub < 24) | has_yhi)

    def masked(v, j):
        keep = inside
        if j < halo:
            keep = inside & has_xlo
        elif j >= halo + nx:
            keep = inside & has_xhi
        return jnp.where(keep, v, 0.0)

    src = []
    for j in range(rows):
        lowp = fromlow[j]
        highp = fromhigh[j]
        x = j - halo
        if 0 <= x < nx:
            first, last = prov[1, x, 0:1], prov[1, x, 15:16]
        else:
            first, last = edge_rows(low_edge if x < 0 else high_edge, j if x < 0 else x - nx)
        low1 = jnp.where(has_ylo, lowp[1:2], 0.0)
        high1 = jnp.where(has_yhi, highp[6:7], 0.0)
        value = jnp.concatenate([lowp, source[j], highp], axis=0)
        add = jnp.where(sub == 7, jnp.broadcast_to(first, (32, 128)), 0.0)
        add = jnp.where(sub == 8, jnp.broadcast_to(-low1, (32, 128)), add)
        add = jnp.where(sub == 23, jnp.broadcast_to(high1, (32, 128)), add)
        add = jnp.where(sub == 24, jnp.broadcast_to(-last, (32, 128)), add)
        value = masked((value + add) * (1.0 / 6.0), j)
        src.append(value)
        pa[j] = -value
    cur, new = pa, pb
    for sweep in range(1, 4):
        for j in range(sweep, rows - sweep):
            here = cur[j]
            up, down = zshift(here, lane)
            total = (cur[j - 1] + cur[j + 1]) + (pltpu.roll(here, 1, 0) + pltpu.roll(here, 31, 0))
            total = total + (up + down)
            new[j] = masked(total * (1.0 / 6.0) - src[j], j)
        cur, new = new, cur
    return cur, halo


def step_kernel(prov, x1, x2, source, y1, y2, spread, prov2, source2, out1, out2, pa, pb, ux, xlo, xhi, fromlow, fromhigh, tolow, tohigh):
    pick(x1, x2, xlo, xhi, "gx")
    pick(y1, y2, fromlow, fromhigh, "gy")
    nx = prov.shape[1]
    p, halo = solve(prov, xlo, xhi, source, fromlow, fromhigh, pa, pb)
    has_xlo, has_xhi, has_ylo, has_yhi = edge_flags()
    sub = lax.broadcasted_iota(jnp.int32, (32, 128), 0)
    lane = lax.broadcasted_iota(jnp.int32, (32, 128), 1)
    inside = ((sub >= 8) | has_ylo) & ((sub < 24) | has_yhi)
    for x in range(-1, nx + 1):
        j = x + halo
        here = p[j]
        up, down = zshift(here, lane)
        slopes = (
            p[j + 1] - p[j - 1],
            pltpu.roll(here, 31, 0) - pltpu.roll(here, 1, 0),
            up - down,
        )
        keep = inside
        if x < 0:
            keep = inside & has_xlo
        elif x >= nx:
            keep = inside & has_xhi
        lowp, highp = fromlow[j], fromhigh[j]
        for c in range(3):
            mid = xlo[halo + c] if x < 0 else xhi[halo + c] if x >= nx else prov[c, x]
            wide = jnp.concatenate(
                [pltpu.roll(lowp, 7 - c, 0), mid, pltpu.roll(highp, 3 - c, 0)], axis=0
            )
            ux[c, x + 1] = jnp.where(keep, wide - 0.25 * slopes[c], 0.0)
    lane16 = lax.broadcasted_iota(jnp.int32, (16, 128), 1)
    for c in range(3):
        for x in range(nx):
            here = ux[c, x + 1]
            ys = pltpu.roll(here, 1, 0) + pltpu.roll(here, 31, 0)
            mid = here[8:24]
            up, down = zshift(mid, lane16)
            total = (ux[c, x, 8:24] + ux[c, x + 2, 8:24]) + ys[8:24] + (up + down)
            pull = spread[c, x] - spread[3, x] * mid
            value = mid + 0.5 * (0.2 * (total - 6.0 * mid) + pull)
            prov2[c, x] = value
    divergence(lambda c, x: prov2[c, x], nx, source2, tolow, tohigh, (0,))
    place(tolow, tohigh, out1, out2, "gx")


def step_call(prov, xlo, xhi, source, fromlow, fromhigh, spread):
    _, nx, ny, nz = prov.shape
    rows = source.shape[0]
    return pl.pallas_call(
        step_kernel,
        out_shape=(
            jax.ShapeDtypeStruct(prov.shape, F32),
            jax.ShapeDtypeStruct((nx, ny, nz), F32),
            jax.ShapeDtypeStruct((HALO2 + 2, ny, nz), F32),
            jax.ShapeDtypeStruct((HALO2 + 2, ny, nz), F32),
        ),
        in_specs=[pl.BlockSpec(memory_space=VMEM)] * 7,
        out_specs=(pl.BlockSpec(memory_space=VMEM),) * 4,
        scratch_shapes=[
            VMEM((rows, 32, nz), F32),
            VMEM((rows, 32, nz), F32),
            VMEM((3, nx + 2, 32, nz), F32),
        ]
        + [VMEM(xlo.shape, F32)] * 2
        + [VMEM(fromlow.shape, F32)] * 2
        + [VMEM((HALO2 + 2, ny, nz), F32)] * 2,
        compiler_params=pltpu.CompilerParams(vmem_limit_bytes=12 << 20),
        name="step",
    )(prov, xlo, xhi, source, fromlow, fromhigh, spread)


DENSE, SPARSE = 11, 5


def last_kernel(prov, x1, x2, source, y1, y2, arrived, vel, picked, pa, pb, table, xlo, xhi, fromlow, fromhigh):
    pick(x1, x2, xlo, xhi, "gx")
    pick(y1, y2, fromlow, fromhigh, "gy")
    nx = prov.shape[1]
    senders = arrived.shape[0]
    p, halo = solve(prov, xlo, xhi, source, fromlow, fromhigh, pa, pb)
    lane16 = lax.broadcasted_iota(jnp.int32, (16, 128), 1)
    for x in range(nx):
        j = x + halo
        here = p[j]
        mid = here[8:24]
        up, down = zshift(mid, lane16)
        slopes = (
            p[j + 1, 8:24] - p[j - 1, 8:24],
            (pltpu.roll(here, 31, 0) - pltpu.roll(here, 1, 0))[8:24],
            up - down,
        )
        for c in range(3):
            value = prov[c, x] - 0.25 * slopes[c]
            vel[c, x] = value
            hi, lo = split(value)
            r = 64 * c + 16 * (x % 4)
            k = 128 * (x // 4)
            table[r : r + 16, k : k + 128] = hi
            table[192 + r : 192 + r + 16, k : k + 128] = lo
    rows8 = lax.broadcasted_iota(jnp.int32, (8, 128), 0)
    iota_r = lax.broadcasted_iota(jnp.int32, (256, 128), 0).astype(F32).astype(BF16)
    iota_c = lax.broadcasted_iota(jnp.int32, (64, 128), 0)
    one, zero = jnp.ones((), BF16), jnp.zeros((), BF16)

    def dense(first):
        hot, cols = [], []
        for s in range(DENSE):
            number = arrived[first + s].astype(jnp.int32)
            rowf = ((number >> 13) * 128 + (number & 127)).astype(F32)
            col = (number >> 7) & 63
            for e in range(2):
                q = 4 * e + 3
                rr = jnp.broadcast_to(rowf[q : q + 1], (256, 128)).astype(BF16)
                hot.append(jnp.where(iota_r == rr, one, zero))
                cols.append(col[q : q + 1])
        got = jnp.dot(table[...], jnp.concatenate(hot, axis=1), preferred_element_type=F32)
        for s in range(DENSE):
            for e in range(2):
                k = 128 * (2 * s + e)
                mask = iota_c == jnp.broadcast_to(cols[2 * s + e], (64, 128))
                for c in range(3):
                    val = got[64 * c : 64 * c + 64, k : k + 128] + got[192 + 64 * c : 256 + 64 * c, k : k + 128]
                    val = jnp.where(mask, val, 0.0)
                    picked[2 * (first + s) + e, :, 128 * c : 128 * c + 128] = jnp.sum(val, axis=0, keepdims=True)

    def sparse(first):
        for s in range(SPARSE):
            number = arrived[first + s].astype(jnp.int32)
            for e in range(2):
                q = 4 * e + 3
                cell = jnp.broadcast_to(number[q : q + 1], (8, 128))
                z = cell & 127
                column = (cell >> 7) - rows8
                acc = [jnp.zeros((8, 128), F32) for _ in range(3)]
                for g in range(2 * nx):
                    mask = column == 8 * g
                    for c in range(3):
                        field = vel[c, g // 2, 8 * (g % 2) : 8 * (g % 2) + 8, :]
                        got = jnp.take_along_axis(field, z, axis=1, mode="promise_in_bounds")
                        acc[c] = jnp.where(mask, got, acc[c])
                for c in range(3):
                    picked[2 * (first + s) + e, :, 128 * c : 128 * c + 128] = jnp.sum(acc[c], axis=0, keepdims=True)

    def loop(i, carry):
        first = i * (DENSE + SPARSE)
        sparse(first)
        dense(first + SPARSE)
        return carry

    lax.fori_loop(0, senders // (DENSE + SPARSE), loop, 0)


def last_call(prov, xlo, xhi, source, fromlow, fromhigh, arrived):
    _, nx, ny, nz = prov.shape
    rows = source.shape[0]
    return pl.pallas_call(
        last_kernel,
        out_shape=(
            jax.ShapeDtypeStruct(prov.shape, F32),
            jax.ShapeDtypeStruct((2 * arrived.shape[0], 1, 3 * nz), F32),
        ),
        in_specs=[pl.BlockSpec(memory_space=VMEM)] * 7,
        out_specs=(pl.BlockSpec(memory_space=VMEM),) * 2,
        scratch_shapes=[
            VMEM((rows, 32, nz), F32),
            VMEM((rows, 32, nz), F32),
            VMEM((384, 256), BF16),
        ]
        + [VMEM(xlo.shape, F32)] * 2
        + [VMEM(fromlow.shape, F32)] * 2,
        compiler_params=pltpu.CompilerParams(vmem_limit_bytes=28 << 20),
        name="last",
    )(prov, xlo, xhi, source, fromlow, fromhigh, arrived)


def pairs(axis, second):
    nx, ny = lax.axis_size("gx"), lax.axis_size("gy")
    out = []
    for i in range(nx):
        for j in range(ny):
            k, count = (i, nx) if axis == "gx" else (j, ny)
            other = ((k + 1) ^ 1) - 1 if second else k ^ 1
            if 0 <= other < count:
                to = (other, j) if axis == "gx" else (i, other)
            else:
                to = (i, j ^ 1) if axis == "gx" else (i ^ 1, j)
            out.append((i * ny + j, to[0] * ny + to[1]))
    return out


def swap(first, second, axis):
    both = ("gx", "gy")
    return (
        lax.ppermute(first, both, pairs(axis, False)),
        lax.ppermute(second, both, pairs(axis, True)),
    )


def body(velocity, marker_force, marker_cell, block_brick):
    devices = lax.axis_size("gx") * lax.axis_size("gy")
    blocks = marker_cell.shape[0]
    axes = ("gx", "gy")
    even_x, even_y = is_even("gx"), is_even("gy")
    outgoing, target = pack(block_brick.reshape(blocks), marker_force, marker_cell, devices)
    low, high = velocity[:, 0], velocity[:, -1]
    first, second = jnp.where(even_x, high, low), jnp.where(even_x, low, high)
    target = jnp.minimum(target, 2 * devices - 1)
    first, second, target = lax.optimization_barrier((first, second, target))
    x1, x2 = swap(first, second, "gx")
    low, high = velocity[:, :, 0], velocity[:, :, -1]
    y1, y2 = swap(jnp.where(even_y, high, low), jnp.where(even_y, low, high), "gy")
    arrived = lax.all_to_all(outgoing, axes, split_axis=0, concat_axis=0, tiled=True)
    prov, spread, brick, out1, out2 = spread_call(arrived, velocity, x1, x2, y1, y2)
    x1, x2 = swap(out1, out2, "gx")
    source, out1, out2 = edges_call(prov, brick, x1, x2, ALL)
    y1, y2 = swap(out1, out2, "gy")
    prov, brick, out1, out2 = step_call(prov, x1, x2, source, y1, y2, spread)
    x1, x2 = swap(out1, out2, "gx")
    source, out1, out2 = edges_call(prov, brick, x1, x2, (0,))
    y1, y2 = swap(out1, out2, "gy")
    final, picked = last_call(prov, x1, x2, source, y1, y2, arrived)
    back = lax.all_to_all(picked, axes, split_axis=0, concat_axis=0, tiled=True)
    return final, unpack(target, back, blocks)


def solution(mesh):
    return jax.shard_map(
        body,
        mesh=mesh,
        in_specs=(
            P(None, "gx", "gy", None),
            P(None, ("gx", "gy"), None),
            P(("gx", "gy"), None),
            P(("gx", "gy"), None),
        ),
        out_specs=(P(None, "gx", "gy", None), P(None, ("gx", "gy"), None)),
        check_vma=False,
    )
```
